32 devices in a mesh: row: 4 (over z), col: 2 (over y), feat: 4 (over x, core).
Axes of the slice: x: 2, y: 2, z: 4, core: 2. Of those that a mesh axis runs over, the one named last changes fastest.
Arguments:
- features: bfloat16 [1024, 1024], P(('row', 'col'), 'feat'), may hold values from -6 to 6
- weight: bfloat16 [1024, 512], replicated, may hold values from -0.1875 to 0.1875
- tile_rows: int32 [4, 2, 128], P('row', 'col', 'feat'), may hold values from 0 to 1
- tile_cols: int32 [4, 2, 128], P('row', 'col', 'feat'), may hold values from 0 to 3
- tile_weights: bfloat16 [4, 2, 128, 128, 128], P('row', 'col', 'feat'), may hold values from -0.078125 to 0.078125
- tile_counts: int32 [4, 2, 4], P('row', 'col', 'feat'), may hold values from 1 to 32, as said below
Outputs:
- aggregated: bfloat16 [1024, 512], P(('row', 'col', 'feat'))
The draws below stay inside these ranges and needn't reach their ends.
Inputs may be any that keep to these rules, and one draw needn't show every extreme that they name: `tile_counts`: at least one device holds exactly 32 live slots.
All inputs are finite; a program needn't handle non-finite values.
Results may differ from the reference program's by a relative error of at most 0.008.
Values may be sent and summed in bfloat16 or wider, within the bound.
A program may use at most 64 MiB of HBM per device.

```python
import math
import jax
import jax.numpy as jnp
import numpy as np
from jax import lax

D_IN = 1024
D_OUT = 512
TILE = 128
PAGES = 128
TILES_DEV = 32
PAGES_ALL = 1024
ROW_TILES = 2
COL_TILES = 4
SLOTS = 128
N_ROW = 4
N_COL = 2
N_FEAT = 4


def draw_tile_counts(key, part):
    key_spread, key_pick = jax.random.split(key)
    total_dev = N_ROW * N_COL * N_FEAT
    spread = jax.random.randint(key_spread, (total_dev,), 0, 8)
    counts = jnp.maximum(TILES_DEV // (1 + spread), 1)
    chosen = jax.random.randint(key_pick, (), 0, total_dev)
    filled = jnp.where(jnp.arange(total_dev) == chosen, TILES_DEV, counts)
    return filled.reshape(N_ROW, N_COL, N_FEAT).astype(jnp.int32)


def set_ends(array, key, low, high):
    spot = [jax.random.randint(jax.random.fold_in(key, axis), (), 0, length) for axis, length in enumerate(array.shape)]
    longest = array.shape.index(max(array.shape))
    neighbour = spot[:longest] + [(spot[longest] + 1) % array.shape[longest]] + spot[longest + 1:]
    return array.at[tuple(spot)].set(low).at[tuple(neighbour)].set(high)


def block_levels(own_key, shape, pieces, low, top_value):
    def one(axis_at, shards_of):
        steps = jax.random.uniform(jax.random.fold_in(jax.random.fold_in(own_key, 6), axis_at), (shards_of,), jnp.float32, low / len(pieces), top_value / len(pieces))
        return jnp.repeat(jnp.exp(steps), shape[axis_at] // shards_of).reshape((-1,) + (1,) * (len(shape) - axis_at - 1))

    gain = one(*pieces[0])
    for cut in pieces[1:]:
        gain = gain * one(*cut)
    return gain


def cumulative_ranks(number_of, skew):
    loads = [(1 << 20) // math.isqrt(grade ** skew) + 1 for grade in range(1, number_of + 1)]
    deviation = 1 + sum(loads) // (1 << 30)
    return np.cumsum(np.array([max(1, weight // deviation) for weight in loads]))


def ranked(stream_key, extent, number_of, skew):
    grid = cumulative_ranks(number_of, skew)
    pick = jax.random.randint(jax.random.fold_in(stream_key, 1), extent, 0, int(grid[number_of - 1]))
    grade = jnp.searchsorted(jnp.asarray(grid, jnp.int32), pick, side="right")
    return jax.random.permutation(jax.random.fold_in(stream_key, 2), number_of)[grade].astype(jnp.int32)


def centred(rng, dims, scale, most, cuts=(), kind=jnp.bfloat16):
    result = scale * jax.random.normal(rng, dims, jnp.float32)
    if cuts:
        result = result * block_levels(rng, dims, cuts, -0.22, 0.18)
    return jnp.clip(result, -most, most).astype(kind)


def setup_inputs(seed: int = 0) -> dict:
    seeds = jax.random.split(jax.random.key(seed), 7)
    features = centred(seeds[0], (PAGES_ALL, D_IN), 1.0, 6.0, ((0, 8), (1, 4)))
    weight = centred(seeds[1], (D_IN, D_OUT), D_IN ** -0.5, 0.1875)
    tile_rows = set_ends(ranked(seeds[2], (N_ROW, N_COL, SLOTS), ROW_TILES, 2), jax.random.fold_in(seeds[2], 3), 0, ROW_TILES - 1).astype(jnp.int32)
    tile_cols = set_ends(jax.random.randint(seeds[3], (N_ROW, N_COL, SLOTS), 0, COL_TILES), jax.random.fold_in(seeds[3], 1), 0, COL_TILES - 1).astype(jnp.int32)
    tile_weights = centred(seeds[4], (N_ROW, N_COL, SLOTS, TILE, TILE), ((N_FEAT * TILES_DEV * TILE * TILE / (3 * PAGES)) ** -0.5), 0.078125, ((0, 4), (1, 2), (2, 4)))
    tile_counts = draw_tile_counts(jax.random.fold_in(seeds[6], 71), 0)
    return dict(features=features, weight=weight, tile_rows=tile_rows, tile_cols=tile_cols, tile_weights=tile_weights, tile_counts=tile_counts)


def reference(features, weight, tile_rows, tile_cols, tile_weights, tile_counts):
    hidden = jnp.dot(features, weight, preferred_element_type=jnp.float32).astype(jnp.bfloat16)
    out_width = hidden.shape[1]
    by_row = hidden.reshape(N_ROW, N_COL * PAGES, out_width)
    by_col = jnp.transpose(hidden.reshape(N_ROW, N_COL, PAGES, out_width), (1, 0, 2, 3)).reshape(N_COL, N_ROW * PAGES, out_width)
    slot_ids = jnp.arange(SLOTS, dtype=jnp.int32)

    def one_block(totals, block_index):
        forward_all, backward_all = totals
        grid_row = block_index // N_COL
        grid_col = block_index % N_COL
        row_ids = tile_rows[grid_row, grid_col]
        col_ids = tile_cols[grid_row, grid_col]
        limits = tile_counts[grid_row, grid_col][slot_ids // TILES_DEV]
        live_mask = ((slot_ids % TILES_DEV) < limits).astype(jnp.float32)
        weights_live = tile_weights[grid_row, grid_col].astype(jnp.float32) * live_mask[:, None, None]
        source = by_col[grid_col].reshape(COL_TILES, TILE, out_width)[col_ids].astype(jnp.float32)
        target = by_row[grid_row].reshape(ROW_TILES, TILE, out_width)[row_ids].astype(jnp.float32)
        pushed = jnp.einsum("kij,kjf->kif", weights_live, source, precision=lax.Precision.HIGHEST)
        pulled = jnp.einsum("kij,kif->kjf", weights_live, target, precision=lax.Precision.HIGHEST)
        forward_add = jax.ops.segment_sum(pushed, row_ids, num_segments=ROW_TILES).reshape(N_COL * PAGES, out_width)
        backward_add = jax.ops.segment_sum(pulled, col_ids, num_segments=COL_TILES).reshape(N_ROW * PAGES, out_width)
        forward_all = forward_all.at[grid_row].add(forward_add)
        backward_all = backward_all.at[grid_col].add(backward_add)
        return (forward_all, backward_all), None

    start_forward = jnp.zeros((N_ROW, N_COL * PAGES, out_width), jnp.float32)
    start_backward = jnp.zeros((N_COL, N_ROW * PAGES, out_width), jnp.float32)
    blocks = jnp.arange(N_ROW * N_COL, dtype=jnp.int32)
    finals, unused = lax.scan(one_block, (start_forward, start_backward), blocks)
    forward_pages = finals[0].reshape(PAGES_ALL, out_width)
    backward_pages = jnp.transpose(finals[1].reshape(N_COL, N_ROW, PAGES, out_width), (1, 0, 2, 3)).reshape(PAGES_ALL, out_width)
    return (forward_pages + backward_pages).astype(jnp.bfloat16)
```

```python
import functools

import jax
import jax.numpy as jnp
from jax import lax
from jax.experimental import pallas as pl
from jax.experimental.pallas import tpu as pltpu
from jax.sharding import PartitionSpec as P

MESH = pl.DeviceIdType.MESH
GROUP = 8
STRIP = 32


def layer(
    sizes,
    rows_hbm, cols_hbm, count_hbm, x_hbm, w_hbm, t_hbm,
    out_ref,
    rows_ref, cols_ref, count_ref,
    x, w, tiles, part, part_own, part_in, col_side, row_side,
    a_part, a_near, a_pair, a_far, a_all, own, sums, gathered,
    load_sem, h_send, h_recv, n_send, n_recv, x_send, x_recv, g_send, g_recv,
    r_send, r_recv, c_send, c_recv, o_send, o_recv,
):
    n_row, n_col, n_feat = sizes
    row, col, feat = lax.axis_index("row"), lax.axis_index("col"), lax.axis_index("feat")
    me = {"row": row, "col": col, "feat": feat}
    size = {"row": n_row, "col": n_col, "feat": n_feat}

    def peer(axis, step):
        return lax.rem(me[axis] + step, size[axis])

    def remote(to, src, dst, send, recv):
        return pltpu.make_async_remote_copy(
            src_ref=src, dst_ref=dst, send_sem=send, recv_sem=recv,
            device_id=to, device_id_type=MESH,
        )

    slots, tile = tiles.shape[0], tiles.shape[1]
    depth = x.shape[1]
    share = part.shape[2]
    block_rows, half = a_near.shape
    out_rows = out_ref.shape[0]
    f32, bf16 = jnp.float32, jnp.bfloat16

    targets = []
    for s in range(1, n_row):
        targets += [(s, t, {"row": peer("row", s), "feat": peer("feat", t)}) for t in range(n_feat)]
    for s in range(1, n_col):
        targets += [
            (n_row - 1 + s, t, {"col": peer("col", s), "feat": peer("feat", t)})
            for t in range(n_feat)
        ]
    targets += [(0, t, {"feat": peer("feat", t)}) for t in range(1, n_feat)]

    barrier = pltpu.get_barrier_semaphore()
    for _, _, to in reversed(targets):
        pl.semaphore_signal(barrier, inc=1, device_id=to, device_id_type=MESH)

    loads = [
        pltpu.make_async_copy(x_hbm, x, load_sem.at[0]),
        pltpu.make_async_copy(
            w_hbm.at[pl.ds(pl.multiple_of(feat * depth, depth), depth)], w, load_sem.at[1]
        ),
        pltpu.make_async_copy(rows_hbm, rows_ref, load_sem.at[2]),
        pltpu.make_async_copy(cols_hbm, cols_ref, load_sem.at[3]),
        pltpu.make_async_copy(count_hbm, count_ref, load_sem.at[4]),
        pltpu.make_async_copy(t_hbm, tiles, load_sem.at[5]),
    ]
    for load in loads:
        load.start()

    loads[0].wait()
    loads[1].wait()
    for g in range(n_feat):
        value = jnp.dot(x[...], w[:, g * share:(g + 1) * share], preferred_element_type=f32)
        part_own[g] = value
        part[g] = value.astype(bf16)
    for load in loads[2:]:
        load.wait()
    count = count_ref[0, 0, 0]
    row_tiles, col_tiles = n_col, n_row
    strips = tile // STRIP
    per_group = GROUP // row_tiles

    def strip_sum(at, carry):
        group, strip = at // strips, at % strips
        first = pl.multiple_of(strip * STRIP, STRIP)

        def add_slot(k, totals):
            place = cols_ref[0, 0, k] * row_tiles + rows_ref[0, 0, k] - group * GROUP
            place = jnp.where(k < count, place, -1)
            value = tiles[k, pl.ds(first, STRIP), :].astype(f32)
            return tuple(
                total + value * jnp.where(place == q, 1.0, 0.0).astype(f32)
                for q, total in enumerate(totals)
            )

        zeros = tuple(jnp.zeros((STRIP, tile), f32) for _ in range(GROUP))
        totals = lax.fori_loop(0, slots, add_slot, zeros, unroll=8)
        for q in range(GROUP):
            at_col = pl.multiple_of((group * per_group + q // row_tiles) * tile, tile)
            at_row = pl.multiple_of((q % row_tiles) * tile + first, STRIP)
            a_part[pl.ds(at_row, STRIP), pl.ds(at_col, tile)] = totals[q].astype(bf16)
        return carry

    lax.fori_loop(0, strips * (row_tiles * col_tiles // GROUP), strip_sum, 0)

    pl.semaphore_wait(barrier, len(targets))
    h_copies = [
        remote(
            {"feat": peer("feat", s)}, part.at[peer("feat", s)], part_in.at[s],
            h_send.at[s], h_recv.at[s],
        )
        for s in range(1, n_feat)
    ]
    for copy in h_copies:
        copy.start()

    side = feat % 2
    near, far = {"feat": feat + 1 - 2 * side}, {"feat": lax.rem(feat + 2, n_feat)}
    halves = half // tile
    near_cols = [pl.ds(pl.multiple_of((1 - side) * half + i * tile, tile), tile) for i in range(halves)]
    own_cols = [pl.ds(pl.multiple_of(side * half + i * tile, tile), tile) for i in range(halves)]
    spots = [pl.ds(i * tile, tile) for i in range(halves)]
    n_copies = [
        remote(near, a_part.at[:, near_cols[i]], a_near.at[:, spots[i]], n_send.at[i], n_recv.at[i])
        for i in range(halves)
    ]
    x_copies = [
        remote(far, a_pair.at[:, spots[i]], a_far.at[:, spots[i]], x_send.at[i], x_recv.at[i])
        for i in range(halves)
    ]
    g_copies = [
        remote(near, a_all.at[:, own_cols[i]], a_all.at[:, own_cols[i]], g_send.at[i], g_recv.at[i])
        for i in range(halves)
    ]
    for copy in n_copies:
        copy.start()
    for i in range(halves):
        n_copies[i].wait_recv()
        pair = a_part[:, own_cols[i]].astype(f32) + a_near[:, spots[i]].astype(f32)
        a_pair[:, spots[i]] = pair.astype(bf16)
        x_copies[i].start()

    hidden = part_own[feat]
    for s in range(1, n_feat):
        h_copies[s - 1].wait_recv()
        hidden += part_in[s].astype(f32)
    hidden = hidden.astype(bf16)
    in_col = pl.ds(pl.multiple_of(row * tile, tile), tile)
    in_row = pl.ds(pl.multiple_of(col * tile, tile), tile)
    col_side[in_col, :] = hidden
    row_side[in_row, :] = hidden
    r_copies = [
        remote(
            {"row": peer("row", s)}, col_side.at[in_col], col_side.at[in_col],
            r_send.at[s], r_recv.at[s],
        )
        for s in range(1, n_row)
    ]
    c_copies = [
        remote(
            {"col": peer("col", s)}, row_side.at[in_row], row_side.at[in_row],
            c_send.at[s], c_recv.at[s],
        )
        for s in range(1, n_col)
    ]
    for copy in r_copies + c_copies:
        copy.start()

    lanes = pl.ds(pl.multiple_of(feat * share, share), share)

    def gift(slot, t, to):
        rows = pl.ds(pl.multiple_of(peer("feat", t) * out_rows, out_rows), out_rows)
        return remote(
            to, sums.at[slot, rows], gathered.at[slot, :, lanes],
            o_send.at[slot, t], o_recv.at[slot, t],
        )

    def backward(at):
        cols = pl.ds(pl.multiple_of(at * tile, tile), tile)
        value = lax.dot_general(
            a_all[:, cols], row_side[...], (((0,), (0,)), ((), ())), preferred_element_type=f32
        )
        slot = lax.rem(at - row + n_row, n_row)

        @pl.when(slot == 0)
        def _():
            own[...] = value

        @pl.when(slot != 0)
        def _():
            sums[slot] = value.astype(bf16)
            for t in range(n_feat):
                gift(slot, t, {"row": at, "feat": peer("feat", t)}).start()

    for i in range(halves):
        x_copies[i].wait_recv()
        both = a_pair[:, spots[i]].astype(f32) + a_far[:, spots[i]].astype(f32)
        a_all[:, own_cols[i]] = both.astype(bf16)
        g_copies[i].start()
        if i == 0:
            for copy in c_copies:
                copy.wait_recv()
        backward(side * halves + i)
    for i in range(halves):
        g_copies[i].wait_recv()
        backward((1 - side) * halves + i)

    def forward(step):
        at = pl.ds(pl.multiple_of(peer("col", step) * tile, tile), tile)
        return jnp.dot(a_all[at, :], col_side[...], preferred_element_type=f32)

    for copy in r_copies:
        copy.wait_recv()
    o_copies = [gift(*target) for target in targets]
    for s in range(1, n_col):
        sums[n_row - 1 + s] = forward(s).astype(bf16)
        for target, copy in zip(targets, o_copies):
            if target[0] == n_row - 1 + s:
                copy.start()
    sums[0] = (own[...] + forward(0)).astype(bf16)
    for target, copy in zip(targets, o_copies):
        if target[0] == 0:
            copy.start()
    kept = pl.ds(pl.multiple_of(feat * out_rows, out_rows), out_rows)
    gathered[0, :, lanes] = sums[0, kept, :]
    for copy in o_copies:
        copy.wait_recv()
    total = gathered[0].astype(f32)
    for slot in range(1, n_row + n_col - 1):
        total += gathered[slot].astype(f32)
    out_ref[...] = total.astype(bf16)
    for copy in h_copies + n_copies + x_copies + g_copies + r_copies + c_copies + o_copies:
        copy.wait_send()


def shards(sizes, features, weight, tile_rows, tile_cols, tile_weights, tile_counts):
    n_row, n_col, n_feat = sizes
    pages, depth = features.shape
    width = weight.shape[1]
    slots, tile = tile_weights.shape[2], tile_weights.shape[3]
    share = width // n_feat
    block_rows, block_cols = n_col * tile, n_row * tile
    half = block_cols // 2
    ways = n_row + n_col - 1
    bf16 = jnp.bfloat16
    dma = pltpu.SemaphoreType.DMA
    hbm = pl.BlockSpec(memory_space=pltpu.HBM)
    vmem = pl.BlockSpec(memory_space=pltpu.VMEM)
    rows_c, cols_c, x_c, w_c, t_c = (pltpu.with_memory_space_constraint(a, pltpu.HBM) for a in (tile_rows, tile_cols, features, weight, tile_weights.reshape(slots, tile, tile)))
    return pl.pallas_call(
        functools.partial(layer, sizes),
        out_shape=jax.ShapeDtypeStruct((pages // n_feat, width), bf16),
        in_specs=[hbm] * 6,
        out_specs=vmem,
        scratch_shapes=[
            pltpu.SMEM(tile_rows.shape, jnp.int32),
            pltpu.SMEM(tile_cols.shape, jnp.int32),
            pltpu.SMEM(tile_counts.shape, jnp.int32),
            pltpu.VMEM((pages, depth), bf16),
            pltpu.VMEM((depth, width), bf16),
            pltpu.VMEM((slots, tile, tile), bf16),
            pltpu.VMEM((n_feat, pages, share), bf16),
            pltpu.VMEM((n_feat, pages, share), jnp.float32),
            pltpu.VMEM((n_feat, pages, share), bf16),
            pltpu.VMEM((block_cols, share), bf16),
            pltpu.VMEM((block_rows, share), bf16),
            pltpu.VMEM((block_rows, block_cols), bf16),
            pltpu.VMEM((block_rows, half), bf16),
            pltpu.VMEM((block_rows, half), bf16),
            pltpu.VMEM((block_rows, half), bf16),
            pltpu.VMEM((block_rows, block_cols), bf16),
            pltpu.VMEM((tile, share), jnp.float32),
            pltpu.VMEM((ways, pages, share), bf16),
            pltpu.VMEM((ways, pages // n_feat, width), bf16),
            dma((6,)),
            dma((n_feat,)), dma((n_feat,)),
            dma((n_row // 2,)), dma((n_row // 2,)),
            dma((n_row // 2,)), dma((n_row // 2,)),
            dma((n_row // 2,)), dma((n_row // 2,)),
            dma((n_row,)), dma((n_row,)),
            dma((n_col,)), dma((n_col,)),
            dma((ways, n_feat)), dma((ways, n_feat)),
        ],
        compiler_params=pltpu.CompilerParams(
            collective_id=0, has_side_effects=True, vmem_limit_bytes=24 * 1024 * 1024
        ),
        name="layer",
    )(rows_c, cols_c, tile_counts, x_c, w_c, t_c)


def solution(mesh):
    sizes = tuple(mesh.shape[axis] for axis in ("row", "col", "feat"))
    placed = (
        P(("row", "col"), "feat"),
        P(),
        P("row", "col", "feat"),
        P("row", "col", "feat"),
        P("row", "col", "feat", None, None),
        P("row", "col", "feat"),
    )
    return jax.shard_map(
        functools.partial(shards, sizes),
        mesh=mesh,
        in_specs=placed,
        out_specs=P(("row", "col", "feat"), None),
        check_vma=False,
    )
```

```python
import functools

import jax
import jax.numpy as jnp
from jax import lax
from jax.experimental import pallas as pl
from jax.experimental.pallas import tpu as pltpu
from jax.sharding import PartitionSpec as P

MESH = pl.DeviceIdType.MESH
GROUP = 8
CHAINS = 2


def layer(
    sizes,
    rows_hbm, cols_hbm, count_hbm, x_hbm, w_hbm, t_hbm,
    out_ref,
    rows_ref, cols_ref, count_ref, prev_ref, last_ref, runs,
    x, w, tiles, part, part_own, part_in, col_side, row_side,
    a_part, a_near, a_pair, a_far, a_all, own, sums, gathered,
    known, load_sem, h_send, h_recv, n_send, n_recv, x_send, x_recv, g_send, g_recv,
    r_send, r_recv, c_send, c_recv, o_send, o_recv,
):
    n_row, n_col, n_feat = sizes
    row, col, feat = lax.axis_index("row"), lax.axis_index("col"), lax.axis_index("feat")
    me = {"row": row, "col": col, "feat": feat}
    size = {"row": n_row, "col": n_col, "feat": n_feat}

    def peer(axis, step):
        return lax.rem(me[axis] + step, size[axis])

    def others(axis):
        at, n = me[axis], size[axis]
        upper = (2 * at) // n
        found = []
        for j in range(n - 1):
            down = n - 1 - j
            down = down - (at - down + n) // n
            up = j + (j - at + n) // n
            found.append((1 - upper) * down + upper * up)
        return found

    def remote(to, src, dst, send, recv):
        return pltpu.make_async_remote_copy(
            src_ref=src, dst_ref=dst, send_sem=send, recv_sem=recv,
            device_id=to, device_id_type=MESH,
        )

    slots, tile = tiles.shape[0], tiles.shape[1]
    depth = x.shape[1]
    share = part.shape[2]
    block_rows, half = a_near.shape
    out_rows = out_ref.shape[0]
    f32, bf16 = jnp.float32, jnp.bfloat16

    targets = []
    for s in range(1, n_row):
        targets += [(s, t, {"row": peer("row", s), "feat": peer("feat", t)}) for t in range(n_feat)]
    for s in range(1, n_col):
        targets += [
            (n_row - 1 + s, t, {"col": peer("col", s), "feat": peer("feat", t)})
            for t in range(n_feat)
        ]
    targets += [(0, t, {"feat": peer("feat", t)}) for t in range(1, n_feat)]

    paired = n_row == 4
    low_bit, high_bit = row % 2, row // 2
    row_1 = row + 1 - 2 * low_bit
    row_2 = row + 2 - 4 * high_bit
    row_3 = row_1 + 2 - 4 * high_bit
    cols_near = [peer("col", s) for s in range(1, n_col)]
    rows_near = [row_1, row_2] if paired else [peer("row", s) for s in range(1, n_row)]
    partners = [{"row": at} for at in rows_near]
    partners += [{"col": at} for at in cols_near]
    partners += [{"feat": peer("feat", t)} for t in range(1, n_feat)]
    barrier = pltpu.get_barrier_semaphore()
    for to in partners:
        pl.semaphore_signal(barrier, inc=1, device_id=to, device_id_type=MESH)

    def announce():
        for i, to in enumerate(partners[:len(rows_near) + len(cols_near)]):
            slot = 1 if paired and i == 1 else 0
            pl.semaphore_signal(known.at[slot], inc=1, device_id=to, device_id_type=MESH)

    def learn_near():
        if paired:
            pl.semaphore_wait(known.at[1], 1)
            pl.semaphore_signal(known.at[2], inc=1, device_id={"row": row_1}, device_id_type=MESH)

    def learn_all():
        pl.semaphore_wait(known.at[0], len(partners) - n_feat + 1 - (1 if paired else 0))
        if paired:
            pl.semaphore_wait(known.at[2], 1)

    loads = [
        pltpu.make_async_copy(x_hbm, x, load_sem.at[0]),
        pltpu.make_async_copy(
            w_hbm.at[pl.ds(pl.multiple_of(feat * depth, depth), depth)], w, load_sem.at[1]
        ),
        pltpu.make_async_copy(rows_hbm, rows_ref, load_sem.at[2]),
        pltpu.make_async_copy(cols_hbm, cols_ref, load_sem.at[3]),
        pltpu.make_async_copy(count_hbm, count_ref, load_sem.at[4]),
        pltpu.make_async_copy(t_hbm, tiles, load_sem.at[5]),
    ]
    for load in loads:
        load.start()

    loads[0].wait()
    loads[1].wait()
    for g in range(n_feat):
        value = jnp.dot(x[...], w[:, g * share:(g + 1) * share], preferred_element_type=f32)
        part_own[g] = value
        part[g] = value.astype(bf16)
    for load in loads[2:5]:
        load.wait()
    count = count_ref[0, 0, 0]
    row_tiles, col_tiles = n_col, n_row
    places = row_tiles * col_tiles
    chain = slots // len(runs)

    def link(k, last):
        place = cols_ref[0, 0, k] * row_tiles + rows_ref[0, 0, k]
        live = jnp.where(k < count, place, -1)
        before = jnp.int32(0)
        for q in range(places):
            before = jnp.where(place == q, last[q], before)
        prev_ref[k] = before
        return tuple(jnp.where(live == q, k % chain + 1, last[q]) for q in range(places))

    for c, run in enumerate(runs):
        run[0] = jnp.zeros((tile, tile), f32)
        last = lax.fori_loop(
            c * chain, (c + 1) * chain, link, (jnp.int32(0),) * places, unroll=chain if places <= GROUP else 1
        )
        for q in range(places):
            last_ref[c * places + q] = last[q]
    loads[5].wait()

    def add_slots(k, carry):
        values = [
            tiles[c * chain + k].astype(f32) + run[prev_ref[c * chain + k]]
            for c, run in enumerate(runs)
        ]
        for run, value in zip(runs, values):
            run[k + 1] = value
        return carry

    lax.fori_loop(0, chain, add_slots, 0, unroll=4)

    def place_sum(q, carry):
        value = runs[0][last_ref[q]]
        for c in range(1, len(runs)):
            value += runs[c][last_ref[c * places + q]]
        at_col = pl.multiple_of((q // row_tiles) * tile, tile)
        at_row = pl.multiple_of((q % row_tiles) * tile, tile)
        a_part[pl.ds(at_row, tile), pl.ds(at_col, tile)] = value.astype(bf16)
        return carry

    lax.fori_loop(0, places, place_sum, 0, unroll=GROUP)

    pl.semaphore_wait(barrier, len(partners))
    h_copies = [
        remote(
            {"feat": peer("feat", s)}, part.at[peer("feat", s)], part_in.at[s],
            h_send.at[s], h_recv.at[s],
        )
        for s in range(1, n_feat)
    ]
    for copy in h_copies:
        copy.start()
    announce()

    side = feat % 2
    near, far = {"feat": feat + 1 - 2 * side}, {"feat": lax.rem(feat + 2, n_feat)}
    halves = half // tile
    near_cols = [pl.ds(pl.multiple_of((1 - side) * half + i * tile, tile), tile) for i in range(halves)]
    own_cols = [pl.ds(pl.multiple_of(side * half + i * tile, tile), tile) for i in range(halves)]
    spots = [pl.ds(i * tile, tile) for i in range(halves)]
    n_copies = [
        remote(near, a_part.at[:, near_cols[i]], a_near.at[:, spots[i]], n_send.at[i], n_recv.at[i])
        for i in range(halves)
    ]
    x_copies = [
        remote(far, a_pair.at[:, spots[i]], a_far.at[:, spots[i]], x_send.at[i], x_recv.at[i])
        for i in range(halves)
    ]
    g_copies = [
        remote(near, a_all.at[:, own_cols[i]], a_all.at[:, own_cols[i]], g_send.at[i], g_recv.at[i])
        for i in range(halves)
    ]
    for copy in n_copies:
        copy.start()
    for i in range(halves):
        n_copies[i].wait_recv()
        pair = a_part[:, own_cols[i]].astype(f32) + a_near[:, spots[i]].astype(f32)
        a_pair[:, spots[i]] = pair.astype(bf16)
        x_copies[i].start()

    learn_near()
    hidden = part_own[feat]
    for s in range(1, n_feat):
        h_copies[s - 1].wait_recv()
        hidden += part_in[s].astype(f32)
    hidden = hidden.astype(bf16)
    in_col = pl.ds(pl.multiple_of(row * tile, tile), tile)
    in_row = pl.ds(pl.multiple_of(col * tile, tile), tile)
    col_side[in_col, :] = hidden
    row_side[in_row, :] = hidden
    r_copies = [
        remote(
            {"row": peer("row", s)}, col_side.at[in_col], col_side.at[in_col],
            r_send.at[s], r_recv.at[s],
        )
        for s in range(1, n_row)
    ]
    c_copies = [
        remote(
            {"col": peer("col", s)}, row_side.at[in_row], row_side.at[in_row],
            c_send.at[s], c_recv.at[s],
        )
        for s in range(1, n_col)
    ]
    learn_all()
    for at in others("row"):
        s = lax.rem(at - row + n_row, n_row)
        remote({"row": at}, col_side.at[in_col], col_side.at[in_col], r_send.at[s], r_recv.at[s]).start()
    for copy in c_copies:
        copy.start()

    lanes = pl.ds(pl.multiple_of(feat * share, share), share)

    def gift(slot, t, to):
        rows = pl.ds(pl.multiple_of(peer("feat", t) * out_rows, out_rows), out_rows)
        return remote(
            to, sums.at[slot, rows], gathered.at[slot, :, lanes],
            o_send.at[slot, t], o_recv.at[slot, t],
        )

    def backward(at):
        cols = pl.ds(pl.multiple_of(at * tile, tile), tile)
        value = lax.dot_general(
            a_all[:, cols], row_side[...], (((0,), (0,)), ((), ())), preferred_element_type=f32
        )
        slot = lax.rem(at - row + n_row, n_row)

        @pl.when(slot == 0)
        def _():
            own[...] = value

        @pl.when(slot != 0)
        def _():
            sums[slot] = value.astype(bf16)
            for t in range(n_feat):
                gift(slot, t, {"row": at, "feat": peer("feat", t)}).start()

    for i in range(halves):
        x_copies[i].wait_recv()
        both = a_pair[:, spots[i]].astype(f32) + a_far[:, spots[i]].astype(f32)
        a_all[:, own_cols[i]] = both.astype(bf16)
        g_copies[i].start()
        if i == 0:
            for copy in c_copies:
                copy.wait_recv()
        backward(side * halves + i)
    for i in range(halves):
        g_copies[i].wait_recv()
        backward((1 - side) * halves + i)

    def forward(step):
        at = pl.ds(pl.multiple_of(peer("col", step) * tile, tile), tile)
        return jnp.dot(a_all[at, :], col_side[...], preferred_element_type=f32)

    for copy in r_copies:
        copy.wait_recv()
    o_copies = [gift(*target) for target in targets]
    for s in range(1, n_col):
        sums[n_row - 1 + s] = forward(s).astype(bf16)
        for target, copy in zip(targets, o_copies):
            if target[0] == n_row - 1 + s:
                copy.start()
    sums[0] = (own[...] + forward(0)).astype(bf16)
    for target, copy in zip(targets, o_copies):
        if target[0] == 0:
            copy.start()
    kept = pl.ds(pl.multiple_of(feat * out_rows, out_rows), out_rows)
    gathered[0, :, lanes] = sums[0, kept, :]
    for copy in o_copies:
        copy.wait_recv()
    total = gathered[0].astype(f32)
    for slot in range(1, n_row + n_col - 1):
        total += gathered[slot].astype(f32)
    out_ref[...] = total.astype(bf16)
    for copy in h_copies + n_copies + x_copies + g_copies + r_copies + c_copies + o_copies:
        copy.wait_send()


def shards(sizes, features, weight, tile_rows, tile_cols, tile_weights, tile_counts):
    n_row, n_col, n_feat = sizes
    pages, depth = features.shape
    width = weight.shape[1]
    slots, tile = tile_weights.shape[2], tile_weights.shape[3]
    share = width // n_feat
    block_rows, block_cols = n_col * tile, n_row * tile
    half = block_cols // 2
    ways = n_row + n_col - 1
    bf16 = jnp.bfloat16
    dma = pltpu.SemaphoreType.DMA
    hbm = pl.BlockSpec(memory_space=pltpu.HBM)
    vmem = pl.BlockSpec(memory_space=pltpu.VMEM)
    rows_c, cols_c, x_c, w_c, t_c = (pltpu.with_memory_space_constraint(a, pltpu.HBM) for a in (tile_rows, tile_cols, features, weight, tile_weights.reshape(slots, tile, tile)))
    return pl.pallas_call(
        functools.partial(layer, sizes),
        out_shape=jax.ShapeDtypeStruct((pages // n_feat, width), bf16),
        in_specs=[hbm] * 6,
        out_specs=vmem,
        scratch_shapes=[
            pltpu.SMEM(tile_rows.shape, jnp.int32),
            pltpu.SMEM(tile_cols.shape, jnp.int32),
            pltpu.SMEM(tile_counts.shape, jnp.int32),
            pltpu.SMEM((slots,), jnp.int32),
            pltpu.SMEM((CHAINS * n_row * n_col,), jnp.int32),
            [pltpu.VMEM((slots // CHAINS + 1, tile, tile), jnp.float32)] * CHAINS,
            pltpu.VMEM((pages, depth), bf16),
            pltpu.VMEM((depth, width), bf16),
            pltpu.VMEM((slots, tile, tile), bf16),
            pltpu.VMEM((n_feat, pages, share), bf16),
            pltpu.VMEM((n_feat, pages, share), jnp.float32),
            pltpu.VMEM((n_feat, pages, share), bf16),
            pltpu.VMEM((block_cols, share), bf16),
            pltpu.VMEM((block_rows, share), bf16),
            pltpu.VMEM((block_rows, block_cols), bf16),
            pltpu.VMEM((block_rows, half), bf16),
            pltpu.VMEM((block_rows, half), bf16),
            pltpu.VMEM((block_rows, half), bf16),
            pltpu.VMEM((block_rows, block_cols), bf16),
            pltpu.VMEM((tile, share), jnp.float32),
            pltpu.VMEM((ways, pages, share), bf16),
            pltpu.VMEM((ways, pages // n_feat, width), bf16),
            pltpu.SemaphoreType.REGULAR((3,)),
            dma((6,)),
            dma((n_feat,)), dma((n_feat,)),
            dma((n_row // 2,)), dma((n_row // 2,)),
            dma((n_row // 2,)), dma((n_row // 2,)),
            dma((n_row // 2,)), dma((n_row // 2,)),
            dma((n_row,)), dma((n_row,)),
            dma((n_col,)), dma((n_col,)),
            dma((ways, n_feat)), dma((ways, n_feat)),
        ],
        compiler_params=pltpu.CompilerParams(
            collective_id=0, has_side_effects=True, vmem_limit_bytes=24 * 1024 * 1024
        ),
        name="layer",
    )(rows_c, cols_c, tile_counts, x_c, w_c, t_c)


def solution(mesh):
    sizes = tuple(mesh.shape[axis] for axis in ("row", "col", "feat"))
    placed = (
        P(("row", "col"), "feat"),
        P(),
        P("row", "col", "feat"),
        P("row", "col", "feat"),
        P("row", "col", "feat", None, None),
        P("row", "col", "feat"),
    )
    return jax.shard_map(
        functools.partial(shards, sizes),
        mesh=mesh,
        in_specs=placed,
        out_specs=P(("row", "col", "feat"), None),
        check_vma=False,
    )
```

```python
import functools

import jax
import jax.numpy as jnp
from jax import lax
from jax.experimental import pallas as pl
from jax.experimental.pallas import tpu as pltpu
from jax.sharding import PartitionSpec as P

MESH = pl.DeviceIdType.MESH
GROUP = 8
CHAINS = 2


def layer(
    sizes,
    rows_hbm, cols_hbm, count_hbm, x_hbm, w_hbm, t_hbm,
    out_ref,
    rows_ref, cols_ref, count_ref, prev_ref, last_ref, runs,
    x, w, tiles, part, part_own, part_in, col_side, row_side,
    a_part, a_near, a_pair, a_far, a_all, own, sums, gathered,
    known_up, known_down, whole, load_sem, h_send, h_recv, n_send, n_recv, x_send, x_recv, g_send, g_recv,
    r_send, r_recv, c_send, c_recv, o_send, o_recv,
):
    n_row, n_col, n_feat = sizes
    row, col, feat = lax.axis_index("row"), lax.axis_index("col"), lax.axis_index("feat")
    me = {"row": row, "col": col, "feat": feat}
    size = {"row": n_row, "col": n_col, "feat": n_feat}

    def peer(axis, step):
        return lax.rem(me[axis] + step, size[axis])

    def others(axis):
        at, n = me[axis], size[axis]
        upper = (2 * at) // n
        found = []
        for j in range(n - 1):
            down = n - 1 - j
            down = down - (at - down + n) // n
            up = j + (j - at + n) // n
            found.append((1 - upper) * down + upper * up)
        return found

    def remote(to, src, dst, send, recv):
        return pltpu.make_async_remote_copy(
            src_ref=src, dst_ref=dst, send_sem=send, recv_sem=recv,
            device_id=to, device_id_type=MESH,
        )

    slots, tile = tiles.shape[0], tiles.shape[1]
    pages, depth = x.shape
    share = part.shape[2]
    block_rows, half = a_near.shape
    out_rows = out_ref.shape[0]
    f32, bf16 = jnp.float32, jnp.bfloat16

    targets = []
    for s in range(1, n_row):
        targets += [(s, t, {"row": peer("row", s), "feat": peer("feat", t)}) for t in range(n_feat)]
    for s in range(1, n_col):
        targets += [
            (n_row - 1 + s, t, {"col": peer("col", s), "feat": peer("feat", t)})
            for t in range(n_feat)
        ]
    targets += [(0, t, {"feat": peer("feat", t)}) for t in range(1, n_feat)]

    below, above = row - 1, row + 1
    has_below, has_above = row > 0, row < n_row - 1
    partners = [{"feat": peer("feat", t)} for t in range(1, n_feat)]
    partners += [{"col": peer("col", s)} for s in range(1, n_col)]
    greeted = len(partners) + jnp.where(has_below, 1, 0) + jnp.where(has_above, 1, 0)
    def signal(sem, to):
        pl.semaphore_signal(sem, inc=1, device_id=to, device_id_type=MESH)

    def announce():
        @pl.when(has_below & has_above)
        def _():
            signal(known_up.at[2], {"row": above})
            signal(known_down.at[2], {"row": below})

    def hand_on():
        for j in range(2, n_row - 1):
            @pl.when((row >= j) & has_above)
            def _():
                pl.semaphore_wait(known_up.at[j], 1)
                signal(known_up.at[j + 1], {"row": above})

            @pl.when((row + j < n_row) & has_below)
            def _():
                pl.semaphore_wait(known_down.at[j], 1)
                signal(known_down.at[j + 1], {"row": below})

    def learn():
        for j in range(2, n_row):
            @pl.when((row >= j) & (row == n_row - 1))
            def _():
                pl.semaphore_wait(known_up.at[j], 1)

            @pl.when((row + j < n_row) & (row == 0))
            def _():
                pl.semaphore_wait(known_down.at[j], 1)
        for s in range(1, n_row):
            signal(whole, {"row": peer("row", s)})
        for s in range(1, n_col):
            signal(whole, {"col": peer("col", s)})

    loads = [
        pltpu.make_async_copy(x_hbm, x, load_sem.at[0]),
        pltpu.make_async_copy(
            w_hbm.at[pl.ds(pl.multiple_of(feat * depth, depth), depth)], w, load_sem.at[1]
        ),
        pltpu.make_async_copy(rows_hbm, rows_ref, load_sem.at[2]),
        pltpu.make_async_copy(cols_hbm, cols_ref, load_sem.at[3]),
        pltpu.make_async_copy(count_hbm, count_ref, load_sem.at[4]),
        pltpu.make_async_copy(t_hbm, tiles, load_sem.at[5]),
    ]
    for load in loads[:2]:
        load.start()
    barrier = pltpu.get_barrier_semaphore()
    for to in partners:
        signal(barrier, to)

    @pl.when(has_below)
    def _():
        signal(barrier, {"row": below})

    @pl.when(has_above)
    def _():
        signal(barrier, {"row": above})

    for load in loads[2:]:
        load.start()

    loads[0].wait()
    loads[1].wait()

    def h_copy(s):
        to = peer("feat", s)
        return remote({"feat": to}, part.at[to], part_in.at[s], h_send.at[0], h_recv.at[0])

    def bytes_of(ref, sem):
        return pltpu.make_async_copy(ref, ref, sem)

    def product(s):
        lanes = pl.ds(pl.multiple_of(peer("feat", s) * share, share), share)
        return jnp.dot(x[...], w[:, lanes], preferred_element_type=f32)

    h_order = [2, 1, 3] if n_feat == 4 else list(range(1, n_feat))
    for s in h_order:
        part[peer("feat", s)] = product(s).astype(bf16)
    pl.semaphore_wait(barrier, greeted)
    for s in h_order:
        h_copy(s).start()
    announce()
    part_own[...] = product(0)
    for load in loads[2:5]:
        load.wait()
    count = count_ref[0, 0, 0]
    row_tiles, col_tiles = n_col, n_row
    places = row_tiles * col_tiles
    chain = slots // len(runs)

    def link(k, last):
        place = cols_ref[0, 0, k] * row_tiles + rows_ref[0, 0, k]
        live = jnp.where(k < count, place, -1)
        before = jnp.int32(0)
        for q in range(places):
            before = jnp.where(place == q, last[q], before)
        prev_ref[k] = before
        return tuple(jnp.where(live == q, k % chain + 1, last[q]) for q in range(places))

    for c, run in enumerate(runs):
        run[0] = jnp.zeros((tile, tile), f32)
        last = lax.fori_loop(
            c * chain, (c + 1) * chain, link, (jnp.int32(0),) * places, unroll=chain if places <= GROUP else 1
        )
        for q in range(places):
            last_ref[c * places + q] = last[q]
    loads[5].wait()

    def add_slots(k, carry):
        values = [
            tiles[c * chain + k].astype(f32) + run[prev_ref[c * chain + k]]
            for c, run in enumerate(runs)
        ]
        for run, value in zip(runs, values):
            run[k + 1] = value
        return carry

    lax.fori_loop(0, chain, add_slots, 0, unroll=4)

    def place_sum(q, carry):
        value = runs[0][last_ref[q]]
        for c in range(1, len(runs)):
            value += runs[c][last_ref[c * places + q]]
        at_col = pl.multiple_of((q // row_tiles) * tile, tile)
        at_row = pl.multiple_of((q % row_tiles) * tile, tile)
        a_part[pl.ds(at_row, tile), pl.ds(at_col, tile)] = value.astype(bf16)
        return carry

    lax.fori_loop(0, places, place_sum, 0, unroll=GROUP)

    side = feat % 2
    near, far = {"feat": feat + 1 - 2 * side}, {"feat": lax.rem(feat + 2, n_feat)}
    halves = half // tile
    near_cols = [pl.ds(pl.multiple_of((1 - side) * half + i * tile, tile), tile) for i in range(halves)]
    own_cols = [pl.ds(pl.multiple_of(side * half + i * tile, tile), tile) for i in range(halves)]
    spots = [pl.ds(i * tile, tile) for i in range(halves)]
    n_copies = [
        remote(near, a_part.at[:, near_cols[i]], a_near.at[:, spots[i]], n_send.at[i], n_recv.at[i])
        for i in range(halves)
    ]
    x_copies = [
        remote(far, a_pair.at[:, spots[i]], a_far.at[:, spots[i]], x_send.at[i], x_recv.at[i])
        for i in range(halves)
    ]
    g_copies = [
        remote(near, a_all.at[:, own_cols[i]], a_all.at[:, own_cols[i]], g_send.at[i], g_recv.at[i])
        for i in range(halves)
    ]
    for copy in n_copies:
        copy.start()
    for i in range(halves):
        n_copies[i].wait_recv()
        pair = a_part[:, own_cols[i]].astype(f32) + a_near[:, spots[i]].astype(f32)
        a_pair[:, spots[i]] = pair.astype(bf16)
        x_copies[i].start()

    hand_on()
    learn()

    def block(at):
        return pl.ds(pl.multiple_of(at * tile, tile), tile)

    bytes_of(part_in.at[pl.ds(1, n_feat - 1)], h_recv.at[0]).wait()
    hidden = part_own[...]
    for s in range(1, n_feat):
        hidden += part_in[s].astype(f32)
    hidden = hidden.astype(bf16)
    col_side[block(row), :] = hidden
    row_side[block(col), :] = hidden
    for at in others("row"):
        spot = col_side.at[block(row)]
        remote({"row": at}, spot, spot, r_send.at[0], r_recv.at[0]).start()
    for s in range(1, n_col):
        spot = row_side.at[block(col)]
        remote({"col": peer("col", s)}, spot, spot, c_send.at[0], c_recv.at[0]).start()
    r_bytes = col_side.at[pl.ds(0, (n_row - 1) * tile)]
    c_bytes = row_side.at[pl.ds(0, (n_col - 1) * tile)]

    lanes = pl.ds(pl.multiple_of(feat * share, share), share)

    def gift(slot, t, to):
        kind = 0 if isinstance(slot, int) and slot == 0 else 1
        rows = pl.ds(pl.multiple_of(peer("feat", t) * out_rows, out_rows), out_rows)
        return remote(
            to, sums.at[slot, rows], gathered.at[slot, :, lanes],
            o_send.at[kind], o_recv.at[kind],
        )

    def backward(at):
        cols = pl.ds(pl.multiple_of(at * tile, tile), tile)
        value = lax.dot_general(
            a_all[:, cols], row_side[...], (((0,), (0,)), ((), ())), preferred_element_type=f32
        )
        slot = lax.rem(at - row + n_row, n_row)

        @pl.when(slot == 0)
        def _():
            own[...] = value

        @pl.when(slot != 0)
        def _():
            sums[slot] = value.astype(bf16)
            for t in range(n_feat):
                gift(slot, t, {"row": at, "feat": peer("feat", t)}).start()

    for i in range(halves):
        x_copies[i].wait_recv()
        both = a_pair[:, spots[i]].astype(f32) + a_far[:, spots[i]].astype(f32)
        a_all[:, own_cols[i]] = both.astype(bf16)
        g_copies[i].start()
        if i == 0:
            bytes_of(c_bytes, c_recv.at[0]).wait()
            pl.semaphore_wait(whole, n_row + n_col - 2)
        backward(side * halves + i)
    for i in range(halves):
        g_copies[i].wait_recv()
        backward((1 - side) * halves + i)

    def forward(step):
        return jnp.dot(a_all[block(peer("col", step)), :], col_side[...], preferred_element_type=f32)

    bytes_of(r_bytes, r_recv.at[0]).wait()
    for s in range(1, n_col):
        sums[n_row - 1 + s] = forward(s).astype(bf16)
        for target in targets:
            if target[0] == n_row - 1 + s:
                gift(*target).start()
    sums[0] = (own[...] + forward(0)).astype(bf16)
    for target in targets:
        if target[0] == 0:
            gift(*target).start()
    kept = pl.ds(pl.multiple_of(feat * out_rows, out_rows), out_rows)
    gathered[0, :, lanes] = sums[0, kept, :]
    few = pl.ds(0, (n_feat - 1) * out_rows)
    many = pl.ds(1, n_row + n_col - 2)
    bytes_of(part_in.at[pl.ds(1, n_feat - 1)], h_send.at[0]).wait()
    bytes_of(r_bytes, r_send.at[0]).wait()
    bytes_of(c_bytes, c_send.at[0]).wait()
    for copy in n_copies + x_copies + g_copies:
        copy.wait_send()
    bytes_of(sums.at[many], o_send.at[1]).wait()
    bytes_of(sums.at[0, few], o_send.at[0]).wait()
    bytes_of(gathered.at[many], o_recv.at[1]).wait()
    bytes_of(sums.at[0, few], o_recv.at[0]).wait()
    total = gathered[0].astype(f32)
    for slot in range(1, n_row + n_col - 1):
        total += gathered[slot].astype(f32)
    out_ref[...] = total.astype(bf16)


def shards(sizes, features, weight, tile_rows, tile_cols, tile_weights, tile_counts):
    n_row, n_col, n_feat = sizes
    pages, depth = features.shape
    width = weight.shape[1]
    slots, tile = tile_weights.shape[2], tile_weights.shape[3]
    share = width // n_feat
    block_rows, block_cols = n_col * tile, n_row * tile
    half = block_cols // 2
    ways = n_row + n_col - 1
    bf16 = jnp.bfloat16
    dma = pltpu.SemaphoreType.DMA
    hbm = pl.BlockSpec(memory_space=pltpu.HBM)
    vmem = pl.BlockSpec(memory_space=pltpu.VMEM)
    rows_c, cols_c, x_c, w_c, t_c = (pltpu.with_memory_space_constraint(a, pltpu.HBM) for a in (tile_rows, tile_cols, features, weight, tile_weights.reshape(slots, tile, tile)))
    return pl.pallas_call(
        functools.partial(layer, sizes),
        out_shape=jax.ShapeDtypeStruct((pages // n_feat, width), bf16),
        in_specs=[hbm] * 6,
        out_specs=vmem,
        scratch_shapes=[
            pltpu.SMEM(tile_rows.shape, jnp.int32),
            pltpu.SMEM(tile_cols.shape, jnp.int32),
            pltpu.SMEM(tile_counts.shape, jnp.int32),
            pltpu.SMEM((slots,), jnp.int32),
            pltpu.SMEM((CHAINS * n_row * n_col,), jnp.int32),
            [pltpu.VMEM((slots // CHAINS + 1, tile, tile), jnp.float32)] * CHAINS,
            pltpu.VMEM((pages, depth), bf16),
            pltpu.VMEM((depth, width), bf16),
            pltpu.VMEM((slots, tile, tile), bf16),
            pltpu.VMEM((n_feat, pages, share), bf16),
            pltpu.VMEM((pages, share), jnp.float32),
            pltpu.VMEM((n_feat, pages, share), bf16),
            pltpu.VMEM((block_cols, share), bf16),
            pltpu.VMEM((block_rows, share), bf16),
            pltpu.VMEM((block_rows, block_cols), bf16),
            pltpu.VMEM((block_rows, half), bf16),
            pltpu.VMEM((block_rows, half), bf16),
            pltpu.VMEM((block_rows, half), bf16),
            pltpu.VMEM((block_rows, block_cols), bf16),
            pltpu.VMEM((tile, share), jnp.float32),
            pltpu.VMEM((ways, pages, share), bf16),
            pltpu.VMEM((ways, pages // n_feat, width), bf16),
            pltpu.SemaphoreType.REGULAR((n_row,)),
            pltpu.SemaphoreType.REGULAR((n_row,)),
            pltpu.SemaphoreType.REGULAR,
            dma((6,)),
            dma((1,)), dma((1,)),
            dma((n_row // 2,)), dma((n_row // 2,)),
            dma((n_row // 2,)), dma((n_row // 2,)),
            dma((n_row // 2,)), dma((n_row // 2,)),
            dma((1,)), dma((1,)),
            dma((1,)), dma((1,)),
            dma((2,)), dma((2,)),
        ],
        compiler_params=pltpu.CompilerParams(
            collective_id=0, has_side_effects=True, vmem_limit_bytes=24 * 1024 * 1024
        ),
        name="layer",
    )(rows_c, cols_c, tile_counts, x_c, w_c, t_c)


def solution(mesh):
    sizes = tuple(mesh.shape[axis] for axis in ("row", "col", "feat"))
    placed = (
        P(("row", "col"), "feat"),
        P(),
        P("row", "col", "feat"),
        P("row", "col", "feat"),
        P("row", "col", "feat", None, None),
        P("row", "col", "feat"),
    )
    return jax.shard_map(
        functools.partial(shards, sizes),
        mesh=mesh,
        in_specs=placed,
        out_specs=P(("row", "col", "feat"), None),
        check_vma=False,
    )
```

```python
import functools

import jax
import jax.numpy as jnp
from jax import lax
from jax.experimental import pallas as pl
from jax.experimental.pallas import tpu as pltpu
from jax.sharding import PartitionSpec as P

MESH = pl.DeviceIdType.MESH
GROUP = 8
CHAINS = 2


def layer(
    sizes,
    rows_hbm, cols_hbm, count_ref, x_hbm, w_hbm, t_hbm,
    out_ref,
    rows_ref, cols_ref, prev_ref, last_ref, runs,
    x, w, tiles, part, products, part_in, col_side, row_side,
    a_part, a_near, a_pair, a_far, a_all, own, sums, gathered,
    known_up, known_down, whole, load_sem, h_send, h_recv, n_send, n_recv, x_send, x_recv, g_send, g_recv,
    r_send, r_recv, c_send, c_recv, o_send, o_recv,
):
    n_row, n_col, n_feat = sizes
    row, col, feat = lax.axis_index("row"), lax.axis_index("col"), lax.axis_index("feat")
    me = {"row": row, "col": col, "feat": feat}
    size = {"row": n_row, "col": n_col, "feat": n_feat}

    def peer(axis, step):
        return lax.rem(me[axis] + step, size[axis])

    def others(axis):
        at, n = me[axis], size[axis]
        upper = (2 * at) // n
        found = []
        for j in range(n - 1):
            down = n - 1 - j
            down = down - (at - down + n) // n
            up = j + (j - at + n) // n
            found.append((1 - upper) * down + upper * up)
        return found

    def remote(to, src, dst, send, recv):
        return pltpu.make_async_remote_copy(
            src_ref=src, dst_ref=dst, send_sem=send, recv_sem=recv,
            device_id=to, device_id_type=MESH,
        )

    slots, tile = tiles.shape[0], tiles.shape[1]
    pages, depth = x.shape
    share = part.shape[2]
    block_rows, half = a_near.shape
    out_rows = out_ref.shape[0]
    f32, bf16 = jnp.float32, jnp.bfloat16

    order = [2, 3, 0, 1] if n_feat == 4 else list(range(n_feat))
    if n_feat == 4:
        mate = feat + 1 - 2 * (feat % 2)
        in_feat = [feat, mate, lax.rem(feat + 2, 4), lax.rem(mate + 2, 4)]
    else:
        in_feat = [peer("feat", t) for t in range(n_feat)]

    targets = []
    for s in range(1, n_row):
        targets += [(s, t, {"row": peer("row", s), "feat": in_feat[t]}) for t in order]
    for s in range(1, n_col):
        targets += [
            (n_row - 1 + s, t, {"col": peer("col", s), "feat": in_feat[t]})
            for t in order
        ]
    targets += [(0, t, {"feat": in_feat[t]}) for t in order if t]

    below, above = row - 1, row + 1
    has_below, has_above = row > 0, row < n_row - 1
    partners = [{"feat": in_feat[t]} for t in order if t]
    partners += [{"col": peer("col", s)} for s in range(1, n_col)]
    greeted = len(partners) + jnp.where(has_below, 1, 0) + jnp.where(has_above, 1, 0)
    def signal(sem, to):
        pl.semaphore_signal(sem, inc=1, device_id=to, device_id_type=MESH)

    def announce():
        @pl.when(has_below & has_above)
        def _():
            signal(known_up.at[2], {"row": above})
            signal(known_down.at[2], {"row": below})

    def hand_on():
        for j in range(2, n_row - 1):
            @pl.when((row >= j) & has_above)
            def _():
                pl.semaphore_wait(known_up.at[j], 1)
                signal(known_up.at[j + 1], {"row": above})

            @pl.when((row + j < n_row) & has_below)
            def _():
                pl.semaphore_wait(known_down.at[j], 1)
                signal(known_down.at[j + 1], {"row": below})

    def learn():
        for j in range(2, n_row):
            @pl.when((row >= j) & (row == n_row - 1))
            def _():
                pl.semaphore_wait(known_up.at[j], 1)

            @pl.when((row + j < n_row) & (row == 0))
            def _():
                pl.semaphore_wait(known_down.at[j], 1)
        for s in range(1, n_row):
            signal(whole, {"row": peer("row", s)})
        for s in range(1, n_col):
            signal(whole, {"col": peer("col", s)})

    loads = [
        pltpu.make_async_copy(x_hbm, x, load_sem.at[0]),
        pltpu.make_async_copy(
            w_hbm.at[pl.ds(pl.multiple_of(feat * depth, depth), depth)], w, load_sem.at[1]
        ),
        pltpu.make_async_copy(rows_hbm, rows_ref, load_sem.at[2]),
        pltpu.make_async_copy(cols_hbm, cols_ref, load_sem.at[3]),
        pltpu.make_async_copy(t_hbm, tiles, load_sem.at[4]),
    ]
    barrier = pltpu.get_barrier_semaphore()
    for to in partners[:n_feat - 1]:
        signal(barrier, to)
    for load in (loads[1], loads[0]):
        load.start()
    for to in partners[n_feat - 1:]:
        signal(barrier, to)

    @pl.when(has_below)
    def _():
        signal(barrier, {"row": below})

    @pl.when(has_above)
    def _():
        signal(barrier, {"row": above})

    for load in loads[2:]:
        load.start()

    loads[0].wait()
    loads[1].wait()

    def h_copy(s):
        to = in_feat[s]
        return remote({"feat": to}, part.at[to], part_in.at[s], h_send.at[0], h_recv.at[0])

    def bytes_of(ref, sem):
        return pltpu.make_async_copy(ref, ref, sem)

    h_order = [s for s in order if s]
    value = jnp.dot(x[...], w[...], preferred_element_type=f32)
    for g in range(n_feat):
        part[g] = value[:, g * share:(g + 1) * share].astype(bf16)
        products[g] = value[:, g * share:(g + 1) * share]
    pl.semaphore_wait(barrier, greeted)
    for s in h_order:
        h_copy(s).start()
    announce()
    for load in loads[2:4]:
        load.wait()
    count = count_ref[0, 0, 0]
    row_tiles, col_tiles = n_col, n_row
    places = row_tiles * col_tiles
    chain = slots // len(runs)

    def link(k, last):
        place = cols_ref[0, 0, k] * row_tiles + rows_ref[0, 0, k]
        live = jnp.where(k < count, place, -1)
        before = jnp.int32(0)
        for q in range(places):
            before = jnp.where(place == q, last[q], before)
        prev_ref[k] = before
        return tuple(jnp.where(live == q, k % chain + 1, last[q]) for q in range(places))

    for c, run in enumerate(runs):
        run[0] = jnp.zeros((tile, tile), f32)
        last = lax.fori_loop(
            c * chain, (c + 1) * chain, link, (jnp.int32(0),) * places, unroll=chain if places <= GROUP else 1
        )
        for q in range(places):
            last_ref[c * places + q] = last[q]
    loads[4].wait()

    def add_slots(k, carry):
        values = [
            tiles[c * chain + k].astype(f32) + run[prev_ref[c * chain + k]]
            for c, run in enumerate(runs)
        ]
        for run, value in zip(runs, values):
            run[k + 1] = value
        return carry

    lax.fori_loop(0, chain, add_slots, 0, unroll=4)

    def place_sum(q, carry):
        value = runs[0][last_ref[q]]
        for c in range(1, len(runs)):
            value += runs[c][last_ref[c * places + q]]
        at_col = pl.multiple_of((q // row_tiles) * tile, tile)
        at_row = pl.multiple_of((q % row_tiles) * tile, tile)
        a_part[pl.ds(at_row, tile), pl.ds(at_col, tile)] = value.astype(bf16)
        return carry

    lax.fori_loop(0, places, place_sum, 0, unroll=GROUP)

    side = feat % 2
    near, far = {"feat": feat + 1 - 2 * side}, {"feat": lax.rem(feat + 2, n_feat)}
    halves = half // tile
    near_cols = [pl.ds(pl.multiple_of((1 - side) * half + i * tile, tile), tile) for i in range(halves)]
    own_cols = [pl.ds(pl.multiple_of(side * half + i * tile, tile), tile) for i in range(halves)]
    spots = [pl.ds(i * tile, tile) for i in range(halves)]
    n_copies = [
        remote(near, a_part.at[:, near_cols[i]], a_near.at[:, spots[i]], n_send.at[i], n_recv.at[i])
        for i in range(halves)
    ]
    x_copies = [
        remote(far, a_pair.at[:, spots[i]], a_far.at[:, spots[i]], x_send.at[i], x_recv.at[i])
        for i in range(halves)
    ]
    g_copies = [
        remote(near, a_all.at[:, own_cols[i]], a_all.at[:, own_cols[i]], g_send.at[i], g_recv.at[i])
        for i in range(halves)
    ]
    for copy in n_copies:
        copy.start()
    for i in range(halves):
        n_copies[i].wait_recv()
        pair = a_part[:, own_cols[i]].astype(f32) + a_near[:, spots[i]].astype(f32)
        a_pair[:, spots[i]] = pair.astype(bf16)
        x_copies[i].start()

    hand_on()
    learn()

    def block(at):
        return pl.ds(pl.multiple_of(at * tile, tile), tile)

    bytes_of(part_in.at[pl.ds(1, n_feat - 1)], h_recv.at[0]).wait()
    hidden = products[feat]
    for s in range(1, n_feat):
        hidden += part_in[s].astype(f32)
    hidden = hidden.astype(bf16)
    col_side[block(row), :] = hidden
    row_side[block(col), :] = hidden
    for at in others("row"):
        spot = col_side.at[block(row)]
        remote({"row": at}, spot, spot, r_send.at[0], r_recv.at[0]).start()
    for s in range(1, n_col):
        spot = row_side.at[block(col)]
        remote({"col": peer("col", s)}, spot, spot, c_send.at[0], c_recv.at[0]).start()
    r_bytes = col_side.at[pl.ds(0, (n_row - 1) * tile)]
    c_bytes = row_side.at[pl.ds(0, (n_col - 1) * tile)]

    lanes = pl.ds(pl.multiple_of(feat * share, share), share)

    def gift(slot, t, to):
        kind = 0 if isinstance(slot, int) and slot == 0 else 1
        rows = pl.ds(pl.multiple_of(in_feat[t] * out_rows, out_rows), out_rows)
        return remote(
            to, sums.at[slot, rows], gathered.at[slot, :, lanes],
            o_send.at[kind], o_recv.at[kind],
        )

    def backward(at):
        cols = pl.ds(pl.multiple_of(at * tile, tile), tile)
        value = lax.dot_general(
            a_all[:, cols], row_side[...], (((0,), (0,)), ((), ())), preferred_element_type=f32
        )
        slot = lax.rem(at - row + n_row, n_row)

        @pl.when(slot == 0)
        def _():
            own[...] = value

        @pl.when(slot != 0)
        def _():
            sums[slot] = value.astype(bf16)
            for t in order:
                gift(slot, t, {"row": at, "feat": in_feat[t]}).start()

    for i in range(halves):
        x_copies[i].wait_recv()
        both = a_pair[:, spots[i]].astype(f32) + a_far[:, spots[i]].astype(f32)
        a_all[:, own_cols[i]] = both.astype(bf16)
        g_copies[i].start()
        if i == 0:
            bytes_of(c_bytes, c_recv.at[0]).wait()
            pl.semaphore_wait(whole, n_row + n_col - 2)
        backward(side * halves + i)
    for i in range(halves):
        g_copies[i].wait_recv()
        backward((1 - side) * halves + i)

    def forward(step, at):
        return jnp.dot(
            a_all[block(peer("col", step)), block(at)], col_side[block(at), :], preferred_element_type=f32
        )

    steps = [*range(1, n_col), 0]
    totals = [forward(s, row) for s in steps]
    totals[-1] += own[...]
    bytes_of(r_bytes, r_recv.at[0]).wait()
    for i, s in enumerate(steps):
        for at in others("row"):
            totals[i] += forward(s, at)
        slot = n_row - 1 + s if s else 0
        sums[slot] = totals[i].astype(bf16)
        for target in targets:
            if target[0] == slot:
                gift(*target).start()
    kept = pl.ds(pl.multiple_of(feat * out_rows, out_rows), out_rows)
    gathered[0, :, lanes] = sums[0, kept, :]
    few = pl.ds(0, (n_feat - 1) * out_rows)
    many = pl.ds(1, n_row + n_col - 2)
    bytes_of(part_in.at[pl.ds(1, n_feat - 1)], h_send.at[0]).wait()
    bytes_of(r_bytes, r_send.at[0]).wait()
    bytes_of(c_bytes, c_send.at[0]).wait()
    for copy in n_copies + x_copies + g_copies:
        copy.wait_send()
    bytes_of(sums.at[many], o_send.at[1]).wait()
    bytes_of(sums.at[0, few], o_send.at[0]).wait()
    bytes_of(gathered.at[many], o_recv.at[1]).wait()
    bytes_of(sums.at[0, few], o_recv.at[0]).wait()
    total = gathered[0].astype(f32)
    for slot in range(1, n_row + n_col - 1):
        total += gathered[slot].astype(f32)
    out_ref[...] = total.astype(bf16)


def shards(sizes, features, weight, tile_rows, tile_cols, tile_weights, tile_counts):
    n_row, n_col, n_feat = sizes
    pages, depth = features.shape
    width = weight.shape[1]
    slots, tile = tile_weights.shape[2], tile_weights.shape[3]
    share = width // n_feat
    block_rows, block_cols = n_col * tile, n_row * tile
    half = block_cols // 2
    ways = n_row + n_col - 1
    bf16 = jnp.bfloat16
    dma = pltpu.SemaphoreType.DMA
    hbm = pl.BlockSpec(memory_space=pltpu.HBM)
    vmem = pl.BlockSpec(memory_space=pltpu.VMEM)
    rows_c, cols_c, x_c, w_c, t_c = (pltpu.with_memory_space_constraint(a, pltpu.HBM) for a in (tile_rows, tile_cols, features, weight, tile_weights.reshape(slots, tile, tile)))
    return pl.pallas_call(
        functools.partial(layer, sizes),
        out_shape=jax.ShapeDtypeStruct((pages // n_feat, width), bf16),
        in_specs=[hbm] * 2 + [pl.BlockSpec(memory_space=pltpu.SMEM)] + [hbm] * 3,
        out_specs=vmem,
        scratch_shapes=[
            pltpu.SMEM(tile_rows.shape, jnp.int32),
            pltpu.SMEM(tile_cols.shape, jnp.int32),
            pltpu.SMEM((slots,), jnp.int32),
            pltpu.SMEM((CHAINS * n_row * n_col,), jnp.int32),
            [pltpu.VMEM((slots // CHAINS + 1, tile, tile), jnp.float32)] * CHAINS,
            pltpu.VMEM((pages, depth), bf16),
            pltpu.VMEM((depth, width), bf16),
            pltpu.VMEM((slots, tile, tile), bf16),
            pltpu.VMEM((n_feat, pages, share), bf16),
            pltpu.VMEM((n_feat, pages, share), jnp.float32),
            pltpu.VMEM((n_feat, pages, share), bf16),
            pltpu.VMEM((block_cols, share), bf16),
            pltpu.VMEM((block_rows, share), bf16),
            pltpu.VMEM((block_rows, block_cols), bf16),
            pltpu.VMEM((block_rows, half), bf16),
            pltpu.VMEM((block_rows, half), bf16),
            pltpu.VMEM((block_rows, half), bf16),
            pltpu.VMEM((block_rows, block_cols), bf16),
            pltpu.VMEM((tile, share), jnp.float32),
            pltpu.VMEM((ways, pages, share), bf16),
            pltpu.VMEM((ways, pages // n_feat, width), bf16),
            pltpu.SemaphoreType.REGULAR((n_row,)),
            pltpu.SemaphoreType.REGULAR((n_row,)),
            pltpu.SemaphoreType.REGULAR,
            dma((5,)),
            dma((1,)), dma((1,)),
            dma((n_row // 2,)), dma((n_row // 2,)),
            dma((n_row // 2,)), dma((n_row // 2,)),
            dma((n_row // 2,)), dma((n_row // 2,)),
            dma((1,)), dma((1,)),
            dma((1,)), dma((1,)),
            dma((2,)), dma((2,)),
        ],
        compiler_params=pltpu.CompilerParams(
            collective_id=0, has_side_effects=True, vmem_limit_bytes=24 * 1024 * 1024
        ),
        name="layer",
    )(rows_c, cols_c, tile_counts, x_c, w_c, t_c)


def solution(mesh):
    sizes = tuple(mesh.shape[axis] for axis in ("row", "col", "feat"))
    placed = (
        P(("row", "col"), "feat"),
        P(),
        P("row", "col", "feat"),
        P("row", "col", "feat"),
        P("row", "col", "feat", None, None),
        P("row", "col", "feat"),
    )
    return jax.shard_map(
        functools.partial(shards, sizes),
        mesh=mesh,
        in_specs=placed,
        out_specs=P(("row", "col", "feat"), None),
        check_vma=False,
    )
```

```python
import functools

import jax
import jax.numpy as jnp
from jax import lax
from jax.experimental import pallas as pl
from jax.experimental.pallas import tpu as pltpu
from jax.sharding import PartitionSpec as P

MESH = pl.DeviceIdType.MESH
GROUP = 8
CHAINS = 2


def layer(
    sizes,
    rows_hbm, cols_hbm, count_ref, x_hbm, w_hbm, t_hbm,
    out_ref,
    rows_ref, cols_ref, prev_ref, last_ref, runs,
    x, w, tiles, part, products, part_in, col_side, row_side,
    a_part, a_near, a_pair, a_far, a_all, sums_b, sums_f, gathered,
    known_up, known_down, whole, load_sem, h_send, h_recv, n_send, n_recv, x_send, x_recv, g_send, g_recv,
    r_send, r_recv, c_send, c_recv, o_send, o_recv,
):
    n_row, n_col, n_feat = sizes
    row, col, feat = lax.axis_index("row"), lax.axis_index("col"), lax.axis_index("feat")
    me = {"row": row, "col": col, "feat": feat}
    size = {"row": n_row, "col": n_col, "feat": n_feat}

    def peer(axis, step):
        return lax.rem(me[axis] + step, size[axis])

    def others(axis):
        at, n = me[axis], size[axis]
        upper = (2 * at) // n
        found = []
        for j in range(n - 1):
            down = n - 1 - j
            down = down - (at - down + n) // n
            up = j + (j - at + n) // n
            found.append((1 - upper) * down + upper * up)
        return found

    def remote(to, src, dst, send, recv):
        return pltpu.make_async_remote_copy(
            src_ref=src, dst_ref=dst, send_sem=send, recv_sem=recv,
            device_id=to, device_id_type=MESH,
        )

    slots, tile = tiles.shape[0], tiles.shape[1]
    pages, depth = x.shape
    share = part.shape[2]
    block_rows, half = a_near.shape
    out_rows = out_ref.shape[0]
    f32, bf16 = jnp.float32, jnp.bfloat16

    order = [2, 3, 0, 1] if n_feat == 4 else list(range(n_feat))
    if n_feat == 4:
        mate = feat + 1 - 2 * (feat % 2)
        in_feat = [feat, mate, lax.rem(feat + 2, 4), lax.rem(mate + 2, 4)]
    else:
        in_feat = [peer("feat", t) for t in range(n_feat)]

    below, above = row - 1, row + 1
    has_below, has_above = row > 0, row < n_row - 1
    partners = [{"feat": in_feat[t]} for t in order if t]
    partners += [{"col": peer("col", s)} for s in range(1, n_col)]
    greeted = len(partners) + jnp.where(has_below, 1, 0) + jnp.where(has_above, 1, 0)
    def signal(sem, to):
        pl.semaphore_signal(sem, inc=1, device_id=to, device_id_type=MESH)

    def announce():
        @pl.when(has_below & has_above)
        def _():
            signal(known_up.at[2], {"row": above})
            signal(known_down.at[2], {"row": below})

    def hand_on():
        for j in range(2, n_row - 1):
            @pl.when((row >= j) & has_above)
            def _():
                pl.semaphore_wait(known_up.at[j], 1)
                signal(known_up.at[j + 1], {"row": above})

            @pl.when((row + j < n_row) & has_below)
            def _():
                pl.semaphore_wait(known_down.at[j], 1)
                signal(known_down.at[j + 1], {"row": below})

    def learn():
        for j in range(2, n_row):
            @pl.when((row >= j) & (row == n_row - 1))
            def _():
                pl.semaphore_wait(known_up.at[j], 1)

            @pl.when((row + j < n_row) & (row == 0))
            def _():
                pl.semaphore_wait(known_down.at[j], 1)
        for s in range(1, n_row):
            signal(whole, {"row": peer("row", s)})
        for s in range(1, n_col):
            signal(whole, {"col": peer("col", s)})

    loads = [
        pltpu.make_async_copy(x_hbm, x, load_sem.at[0]),
        pltpu.make_async_copy(
            w_hbm.at[pl.ds(pl.multiple_of(feat * depth, depth), depth)], w, load_sem.at[1]
        ),
        pltpu.make_async_copy(rows_hbm, rows_ref, load_sem.at[2]),
        pltpu.make_async_copy(cols_hbm, cols_ref, load_sem.at[3]),
        pltpu.make_async_copy(t_hbm, tiles, load_sem.at[4]),
    ]
    barrier = pltpu.get_barrier_semaphore()
    for to in partners[:n_feat - 1]:
        signal(barrier, to)
    for load in (loads[1], loads[0]):
        load.start()
    for to in partners[n_feat - 1:]:
        signal(barrier, to)

    @pl.when(has_below)
    def _():
        signal(barrier, {"row": below})

    @pl.when(has_above)
    def _():
        signal(barrier, {"row": above})

    for load in loads[2:]:
        load.start()

    loads[0].wait()
    loads[1].wait()

    def h_copy(s):
        to = in_feat[s]
        return remote({"feat": to}, part.at[to], part_in.at[s], h_send.at[0], h_recv.at[0])

    def bytes_of(ref, sem):
        return pltpu.make_async_copy(ref, ref, sem)

    h_order = [s for s in order if s]
    value = jnp.dot(x[...], w[...], preferred_element_type=f32)
    for g in range(n_feat):
        part[g] = value[:, g * share:(g + 1) * share].astype(bf16)
        products[g] = value[:, g * share:(g + 1) * share]
    pl.semaphore_wait(barrier, greeted)
    for s in h_order:
        h_copy(s).start()
    announce()
    for load in loads[2:4]:
        load.wait()
    count = count_ref[0, 0, 0]
    row_tiles, col_tiles = n_col, n_row
    places = row_tiles * col_tiles
    chain = slots // len(runs)

    def link(k, last):
        place = cols_ref[0, 0, k] * row_tiles + rows_ref[0, 0, k]
        live = jnp.where(k < count, place, -1)
        before = jnp.int32(0)
        for q in range(places):
            before = jnp.where(place == q, last[q], before)
        prev_ref[k] = before
        return tuple(jnp.where(live == q, k % chain + 1, last[q]) for q in range(places))

    for c, run in enumerate(runs):
        run[0] = jnp.zeros((tile, tile), f32)
        last = lax.fori_loop(
            c * chain, (c + 1) * chain, link, (jnp.int32(0),) * places, unroll=chain if places <= GROUP else 1
        )
        for q in range(places):
            last_ref[c * places + q] = last[q]
    loads[4].wait()

    def add_slots(k, carry):
        values = [
            tiles[c * chain + k].astype(f32) + run[prev_ref[c * chain + k]]
            for c, run in enumerate(runs)
        ]
        for run, value in zip(runs, values):
            run[k + 1] = value
        return carry

    lax.fori_loop(0, chain, add_slots, 0, unroll=4)

    def place_sum(q, carry):
        value = runs[0][last_ref[q]]
        for c in range(1, len(runs)):
            value += runs[c][last_ref[c * places + q]]
        at_col = pl.multiple_of((q // row_tiles) * tile, tile)
        at_row = pl.multiple_of((q % row_tiles) * tile, tile)
        a_part[pl.ds(at_row, tile), pl.ds(at_col, tile)] = value.astype(bf16)
        return carry

    lax.fori_loop(0, places, place_sum, 0, unroll=GROUP)

    side = feat % 2
    near, far = {"feat": feat + 1 - 2 * side}, {"feat": lax.rem(feat + 2, n_feat)}
    halves = half // tile
    near_cols = [pl.ds(pl.multiple_of((1 - side) * half + i * tile, tile), tile) for i in range(halves)]
    own_cols = [pl.ds(pl.multiple_of(side * half + i * tile, tile), tile) for i in range(halves)]
    spots = [pl.ds(i * tile, tile) for i in range(halves)]
    n_copies = [
        remote(near, a_part.at[:, near_cols[i]], a_near.at[:, spots[i]], n_send.at[i], n_recv.at[i])
        for i in range(halves)
    ]
    x_copies = [
        remote(far, a_pair.at[:, spots[i]], a_far.at[:, spots[i]], x_send.at[i], x_recv.at[i])
        for i in range(halves)
    ]
    g_copies = [
        remote(near, a_all.at[:, own_cols[i]], a_all.at[:, own_cols[i]], g_send.at[i], g_recv.at[i])
        for i in range(halves)
    ]
    for copy in n_copies:
        copy.start()
    for i in range(halves):
        n_copies[i].wait_recv()
        pair = a_part[:, own_cols[i]].astype(f32) + a_near[:, spots[i]].astype(f32)
        a_pair[:, spots[i]] = pair.astype(bf16)
        x_copies[i].start()

    hand_on()
    learn()

    def block(at):
        return pl.ds(pl.multiple_of(at * tile, tile), tile)

    bytes_of(part_in.at[pl.ds(1, n_feat - 1)], h_recv.at[0]).wait()
    hidden = products[feat]
    for s in range(1, n_feat):
        hidden += part_in[s].astype(f32)
    hidden = hidden.astype(bf16)
    col_side[block(row), :] = hidden
    pair_lanes = pl.ds(pl.multiple_of(side * share, share), share)
    row_side[block(col), pair_lanes] = hidden
    spot = col_side.at[block(row)]
    rising = [j + (j - row + n_row) // n_row for j in range(n_row - 1)]

    def send_row(at):
        s = lax.rem(at - row + n_row, n_row)
        own_spot = col_side.at[block(row)]
        remote({"row": at}, own_spot, own_spot, r_send.at[0], r_recv.at[s]).start()

    for at in rising:
        send_row(at)
    spot = row_side.at[block(col), pair_lanes]
    for s in range(1, n_col):
        for to in (feat, mate):
            remote({"col": peer("col", s), "feat": to}, spot, spot, c_send.at[0], c_recv.at[0]).start()
    m_copy = remote(near, spot, spot, c_send.at[1], c_recv.at[1])
    m_copy.start()
    r_bytes = col_side.at[pl.ds(0, (n_row - 1) * tile)]
    c_bytes = row_side.at[pl.ds(0, (n_col - 1) * tile)]

    def part_of(t):
        return pl.ds(pl.multiple_of(in_feat[t] * out_rows, out_rows), out_rows)

    lanes = pl.ds(pl.multiple_of(feat * share, share), share)
    wide = pl.ds(pl.multiple_of((feat // 2) * 2 * share, 2 * share), 2 * share)
    few = pl.ds(0, (n_feat - 1) * out_rows)
    mine = row // halves == side

    def gift_back(i, slot, t, to, kind):
        return remote(
            to, sums_b.at[i, part_of(t)], gathered.at[slot, :, wide], o_send.at[kind], o_recv.at[kind]
        )

    def gift_on(step, t, to):
        kind = 3 if step else 2
        return remote(
            to, sums_f.at[step, part_of(t)], gathered.at[n_row + step, :, lanes],
            o_send.at[kind], o_recv.at[kind],
        )

    def backward(i):
        at = side * halves + i
        value = lax.dot_general(
            a_all[:, block(at)], row_side[...], (((0,), (0,)), ((), ())), preferred_element_type=f32
        )
        sums_b[i] = value.astype(bf16)
        slot = lax.rem(at - row + n_row, n_row)

        @pl.when(slot == 0)
        def _():
            for t in order:
                if t:
                    gift_back(i, 0, t, {"feat": in_feat[t]}, 0).start()
            gathered[0, :, wide] = sums_b[i, part_of(0), :]

        @pl.when(slot != 0)
        def _():
            for t in order:
                gift_back(i, slot, t, {"row": at, "feat": in_feat[t]}, 1).start()

    for i in range(halves):
        x_copies[i].wait_recv()
        both = a_pair[:, spots[i]].astype(f32) + a_far[:, spots[i]].astype(f32)
        a_all[:, own_cols[i]] = both.astype(bf16)
        g_copies[i].start()
        if i == 0:
            bytes_of(c_bytes, c_recv.at[0]).wait()
            m_copy.wait_recv()
            pl.semaphore_wait(whole, n_row + n_col - 2)
        backward(i)
    for i in range(halves):
        g_copies[i].wait_recv()

    def forward(step, at):
        return jnp.dot(
            a_all[block(peer("col", step)), block(at)], col_side[block(at), :], preferred_element_type=f32
        )

    steps = [*range(1, n_col), 0]

    def give(step, total):
        sums_f[step] = total.astype(bf16)
        for t in order:
            if step:
                gift_on(step, t, {"col": peer("col", step), "feat": in_feat[t]}).start()
            elif t:
                gift_on(step, t, {"feat": in_feat[t]}).start()

    totals = [forward(s, row) for s in steps]
    arrivals = others("row")[::-1]
    for at in arrivals:
        from_at = lax.rem(row - at + n_row, n_row)
        bytes_of(col_side.at[block(at)], r_recv.at[from_at]).wait()
        for i, s in enumerate(steps):
            totals[i] += forward(s, at)
            if at is arrivals[-1]:
                give(s, totals[i])
    gathered[n_row, :, lanes] = sums_f[0, part_of(0), :]
    bytes_of(part_in.at[pl.ds(1, n_feat - 1)], h_send.at[0]).wait()
    bytes_of(r_bytes, r_send.at[0]).wait()
    bytes_of(c_bytes, c_send.at[0]).wait()
    m_copy.wait_send()
    for copy in n_copies + x_copies + g_copies:
        copy.wait_send()

    @pl.when(mine)
    def _():
        bytes_of(sums_b.at[0, few], o_send.at[0]).wait()
        bytes_of(sums_b.at[pl.ds(0, halves - 1)], o_send.at[1]).wait()
        bytes_of(gathered.at[0, :, wide], o_recv.at[0]).wait()

    @pl.when(jnp.logical_not(mine))
    def _():
        bytes_of(sums_b, o_send.at[1]).wait()
        bytes_of(gathered.at[0], o_recv.at[0]).wait()

    later = pl.ds(n_row + 1, n_col - 1)
    bytes_of(sums_f.at[0, few], o_send.at[2]).wait()
    bytes_of(sums_f.at[pl.ds(1, n_col - 1)], o_send.at[3]).wait()
    bytes_of(gathered.at[pl.ds(1, n_row - 1)], o_recv.at[1]).wait()
    bytes_of(sums_f.at[0, few], o_recv.at[2]).wait()
    bytes_of(gathered.at[later], o_recv.at[3]).wait()
    total = gathered[0].astype(f32)
    for slot in range(1, n_row + n_col):
        total += gathered[slot].astype(f32)
    out_ref[...] = total.astype(bf16)


def shards(sizes, features, weight, tile_rows, tile_cols, tile_weights, tile_counts):
    n_row, n_col, n_feat = sizes
    pages, depth = features.shape
    width = weight.shape[1]
    slots, tile = tile_weights.shape[2], tile_weights.shape[3]
    share = width // n_feat
    block_rows, block_cols = n_col * tile, n_row * tile
    half = block_cols // 2
    bf16 = jnp.bfloat16
    dma = pltpu.SemaphoreType.DMA
    hbm = pl.BlockSpec(memory_space=pltpu.HBM)
    vmem = pl.BlockSpec(memory_space=pltpu.VMEM)
    rows_c, cols_c, x_c, w_c, t_c = (pltpu.with_memory_space_constraint(a, pltpu.HBM) for a in (tile_rows, tile_cols, features, weight, tile_weights.reshape(slots, tile, tile)))
    return pl.pallas_call(
        functools.partial(layer, sizes),
        out_shape=jax.ShapeDtypeStruct((pages // n_feat, width), bf16),
        in_specs=[hbm] * 2 + [pl.BlockSpec(memory_space=pltpu.SMEM)] + [hbm] * 3,
        out_specs=vmem,
        scratch_shapes=[
            pltpu.SMEM(tile_rows.shape, jnp.int32),
            pltpu.SMEM(tile_cols.shape, jnp.int32),
            pltpu.SMEM((slots,), jnp.int32),
            pltpu.SMEM((CHAINS * n_row * n_col,), jnp.int32),
            [pltpu.VMEM((slots // CHAINS + 1, tile, tile), jnp.float32)] * CHAINS,
            pltpu.VMEM((pages, depth), bf16),
            pltpu.VMEM((depth, width), bf16),
            pltpu.VMEM((slots, tile, tile), bf16),
            pltpu.VMEM((n_feat, pages, share), bf16),
            pltpu.VMEM((n_feat, pages, share), jnp.float32),
            pltpu.VMEM((n_feat, pages, share), bf16),
            pltpu.VMEM((block_cols, share), bf16),
            pltpu.VMEM((block_rows, 2 * share), bf16),
            pltpu.VMEM((block_rows, block_cols), bf16),
            pltpu.VMEM((block_rows, half), bf16),
            pltpu.VMEM((block_rows, half), bf16),
            pltpu.VMEM((block_rows, half), bf16),
            pltpu.VMEM((block_rows, block_cols), bf16),
            pltpu.VMEM((n_row // 2, pages, 2 * share), bf16),
            pltpu.VMEM((n_col, pages, share), bf16),
            pltpu.VMEM((n_row + n_col, pages // n_feat, width), bf16),
            pltpu.SemaphoreType.REGULAR((n_row,)),
            pltpu.SemaphoreType.REGULAR((n_row,)),
            pltpu.SemaphoreType.REGULAR,
            dma((5,)),
            dma((1,)), dma((1,)),
            dma((n_row // 2,)), dma((n_row // 2,)),
            dma((n_row // 2,)), dma((n_row // 2,)),
            dma((n_row // 2,)), dma((n_row // 2,)),
            dma((1,)), dma((n_row,)),
            dma((2,)), dma((2,)),
            dma((4,)), dma((4,)),
        ],
        compiler_params=pltpu.CompilerParams(
            collective_id=0, has_side_effects=True, vmem_limit_bytes=24 * 1024 * 1024
        ),
        name="layer",
    )(rows_c, cols_c, tile_counts, x_c, w_c, t_c)


def solution(mesh):
    sizes = tuple(mesh.shape[axis] for axis in ("row", "col", "feat"))
    placed = (
        P(("row", "col"), "feat"),
        P(),
        P("row", "col", "feat"),
        P("row", "col", "feat"),
        P("row", "col", "feat", None, None),
        P("row", "col", "feat"),
    )
    return jax.shard_map(
        functools.partial(shards, sizes),
        mesh=mesh,
        in_specs=placed,
        out_specs=P(("row", "col", "feat"), None),
        check_vma=False,
    )
```

```python
import functools

import jax
import jax.numpy as jnp
from jax import lax
from jax.experimental import pallas as pl
from jax.experimental.pallas import tpu as pltpu
from jax.sharding import PartitionSpec as P

MESH = pl.DeviceIdType.MESH
GROUP = 8
CHAINS = 2


def layer(
    sizes,
    rows_hbm, cols_hbm, count_hbm, x_hbm, w_hbm, t_hbm,
    gathered,
    rows_ref, cols_ref, count_ref, prev_ref, last_ref, runs,
    x, w, tiles, part, part_own, part_in, col_side, row_side,
    a_part, a_near, a_pair, a_far, a_all, own, sums,
    known_up, known_down, whole, load_sem, h_send, h_recv, n_send, n_recv, x_send, x_recv, g_send, g_recv,
    r_send, r_recv, c_send, c_recv, o_send, o_recv,
):
    n_row, n_col, n_feat = sizes
    row, col, feat = lax.axis_index("row"), lax.axis_index("col"), lax.axis_index("feat")
    me = {"row": row, "col": col, "feat": feat}
    size = {"row": n_row, "col": n_col, "feat": n_feat}

    def peer(axis, step):
        return lax.rem(me[axis] + step, size[axis])

    def others(axis):
        at, n = me[axis], size[axis]
        upper = (2 * at) // n
        found = []
        for j in range(n - 1):
            down = n - 1 - j
            down = down - (at - down + n) // n
            up = j + (j - at + n) // n
            found.append((1 - upper) * down + upper * up)
        return found

    def remote(to, src, dst, send, recv):
        return pltpu.make_async_remote_copy(
            src_ref=src, dst_ref=dst, send_sem=send, recv_sem=recv,
            device_id=to, device_id_type=MESH,
        )

    slots, tile = tiles.shape[0], tiles.shape[1]
    pages, depth = x.shape
    share = part.shape[2]
    block_rows, half = a_near.shape
    out_rows = gathered.shape[1]
    f32, bf16 = jnp.float32, jnp.bfloat16

    targets = []
    for s in range(1, n_row):
        targets += [(s, t, {"row": peer("row", s), "feat": peer("feat", t)}) for t in range(n_feat)]
    for s in range(1, n_col):
        targets += [
            (n_row - 1 + s, t, {"col": peer("col", s), "feat": peer("feat", t)})
            for t in range(n_feat)
        ]
    targets += [(0, t, {"feat": peer("feat", t)}) for t in range(1, n_feat)]

    below, above = row - 1, row + 1
    has_below, has_above = row > 0, row < n_row - 1
    partners = [{"feat": peer("feat", t)} for t in range(1, n_feat)]
    partners += [{"col": peer("col", s)} for s in range(1, n_col)]
    greeted = len(partners) + jnp.where(has_below, 1, 0) + jnp.where(has_above, 1, 0)
    def signal(sem, to):
        pl.semaphore_signal(sem, inc=1, device_id=to, device_id_type=MESH)

    def announce():
        @pl.when(has_below & has_above)
        def _():
            signal(known_up.at[2], {"row": above})
            signal(known_down.at[2], {"row": below})

    def hand_on():
        for j in range(2, n_row - 1):
            @pl.when((row >= j) & has_above)
            def _():
                pl.semaphore_wait(known_up.at[j], 1)
                signal(known_up.at[j + 1], {"row": above})

            @pl.when((row + j < n_row) & has_below)
            def _():
                pl.semaphore_wait(known_down.at[j], 1)
                signal(known_down.at[j + 1], {"row": below})

    def learn():
        for j in range(2, n_row):
            @pl.when((row >= j) & (row == n_row - 1))
            def _():
                pl.semaphore_wait(known_up.at[j], 1)

            @pl.when((row + j < n_row) & (row == 0))
            def _():
                pl.semaphore_wait(known_down.at[j], 1)
        for s in range(1, n_row):
            signal(whole, {"row": peer("row", s)})
        for s in range(1, n_col):
            signal(whole, {"col": peer("col", s)})

    loads = [
        pltpu.make_async_copy(x_hbm, x, load_sem.at[0]),
        pltpu.make_async_copy(
            w_hbm.at[pl.ds(pl.multiple_of(feat * depth, depth), depth)], w, load_sem.at[1]
        ),
        pltpu.make_async_copy(rows_hbm, rows_ref, load_sem.at[2]),
        pltpu.make_async_copy(cols_hbm, cols_ref, load_sem.at[3]),
        pltpu.make_async_copy(count_hbm, count_ref, load_sem.at[4]),
        pltpu.make_async_copy(t_hbm, tiles, load_sem.at[5]),
    ]
    for load in loads[:2]:
        load.start()
    barrier = pltpu.get_barrier_semaphore()
    for to in partners:
        signal(barrier, to)

    @pl.when(has_below)
    def _():
        signal(barrier, {"row": below})

    @pl.when(has_above)
    def _():
        signal(barrier, {"row": above})

    for load in loads[2:]:
        load.start()

    loads[0].wait()
    loads[1].wait()

    def h_copy(s):
        to = peer("feat", s)
        return remote({"feat": to}, part.at[to], part_in.at[s], h_send.at[0], h_recv.at[0])

    def bytes_of(ref, sem):
        return pltpu.make_async_copy(ref, ref, sem)

    def product(s):
        lanes = pl.ds(pl.multiple_of(peer("feat", s) * share, share), share)
        return jnp.dot(x[...], w[:, lanes], preferred_element_type=f32)

    h_order = [2, 1, 3] if n_feat == 4 else list(range(1, n_feat))
    for s in h_order:
        part[peer("feat", s)] = product(s).astype(bf16)
    pl.semaphore_wait(barrier, greeted)
    for s in h_order:
        h_copy(s).start()
    announce()
    part_own[...] = product(0)
    for load in loads[2:5]:
        load.wait()
    count = count_ref[0, 0, 0]
    row_tiles, col_tiles = n_col, n_row
    places = row_tiles * col_tiles
    chain = slots // len(runs)

    def link(k, last):
        place = cols_ref[0, 0, k] * row_tiles + rows_ref[0, 0, k]
        live = jnp.where(k < count, place, -1)
        before = jnp.int32(0)
        for q in range(places):
            before = jnp.where(place == q, last[q], before)
        prev_ref[k] = before
        return tuple(jnp.where(live == q, k % chain + 1, last[q]) for q in range(places))

    for c, run in enumerate(runs):
        run[0] = jnp.zeros((tile, tile), f32)
        last = lax.fori_loop(
            c * chain, (c + 1) * chain, link, (jnp.int32(0),) * places, unroll=chain if places <= GROUP else 1
        )
        for q in range(places):
            last_ref[c * places + q] = last[q]
    loads[5].wait()

    def add_slots(k, carry):
        values = [
            tiles[c * chain + k].astype(f32) + run[prev_ref[c * chain + k]]
            for c, run in enumerate(runs)
        ]
        for run, value in zip(runs, values):
            run[k + 1] = value
        return carry

    lax.fori_loop(0, chain, add_slots, 0, unroll=4)

    def place_sum(q, carry):
        value = runs[0][last_ref[q]]
        for c in range(1, len(runs)):
            value += runs[c][last_ref[c * places + q]]
        at_col = pl.multiple_of((q // row_tiles) * tile, tile)
        at_row = pl.multiple_of((q % row_tiles) * tile, tile)
        a_part[pl.ds(at_row, tile), pl.ds(at_col, tile)] = value.astype(bf16)
        return carry

    lax.fori_loop(0, places, place_sum, 0, unroll=GROUP)

    side = feat % 2
    near, far = {"feat": feat + 1 - 2 * side}, {"feat": lax.rem(feat + 2, n_feat)}
    halves = half // tile
    near_cols = [pl.ds(pl.multiple_of((1 - side) * half + i * tile, tile), tile) for i in range(halves)]
    own_cols = [pl.ds(pl.multiple_of(side * half + i * tile, tile), tile) for i in range(halves)]
    spots = [pl.ds(i * tile, tile) for i in range(halves)]
    n_copies = [
        remote(near, a_part.at[:, near_cols[i]], a_near.at[:, spots[i]], n_send.at[i], n_recv.at[i])
        for i in range(halves)
    ]
    x_copies = [
        remote(far, a_pair.at[:, spots[i]], a_far.at[:, spots[i]], x_send.at[i], x_recv.at[i])
        for i in range(halves)
    ]
    g_copies = [
        remote(near, a_all.at[:, own_cols[i]], a_all.at[:, own_cols[i]], g_send.at[i], g_recv.at[i])
        for i in range(halves)
    ]
    for copy in n_copies:
        copy.start()
    for i in range(halves):
        n_copies[i].wait_recv()
        pair = a_part[:, own_cols[i]].astype(f32) + a_near[:, spots[i]].astype(f32)
        a_pair[:, spots[i]] = pair.astype(bf16)
        x_copies[i].start()

    hand_on()
    learn()

    def block(at):
        return pl.ds(pl.multiple_of(at * tile, tile), tile)

    bytes_of(part_in.at[pl.ds(1, n_feat - 1)], h_recv.at[0]).wait()
    hidden = part_own[...]
    for s in range(1, n_feat):
        hidden += part_in[s].astype(f32)
    hidden = hidden.astype(bf16)
    col_side[block(row), :] = hidden
    row_side[block(col), :] = hidden
    for at in others("row"):
        spot = col_side.at[block(row)]
        remote({"row": at}, spot, spot, r_send.at[0], r_recv.at[0]).start()
    for s in range(1, n_col):
        spot = row_side.at[block(col)]
        remote({"col": peer("col", s)}, spot, spot, c_send.at[0], c_recv.at[0]).start()
    r_bytes = col_side.at[pl.ds(0, (n_row - 1) * tile)]
    c_bytes = row_side.at[pl.ds(0, (n_col - 1) * tile)]

    lanes = pl.ds(pl.multiple_of(feat * share, share), share)

    def gift(slot, t, to):
        kind = 0 if isinstance(slot, int) and slot == 0 else 1
        rows = pl.ds(pl.multiple_of(peer("feat", t) * out_rows, out_rows), out_rows)
        return remote(
            to, sums.at[slot, rows], gathered.at[slot, :, lanes],
            o_send.at[kind], o_recv.at[kind],
        )

    def backward(at):
        cols = pl.ds(pl.multiple_of(at * tile, tile), tile)
        value = lax.dot_general(
            a_all[:, cols], row_side[...], (((0,), (0,)), ((), ())), preferred_element_type=f32
        )
        slot = lax.rem(at - row + n_row, n_row)

        @pl.when(slot == 0)
        def _():
            own[...] = value

        @pl.when(slot != 0)
        def _():
            sums[slot] = value.astype(bf16)
            for t in range(n_feat):
                gift(slot, t, {"row": at, "feat": peer("feat", t)}).start()

    for i in range(halves):
        x_copies[i].wait_recv()
        both = a_pair[:, spots[i]].astype(f32) + a_far[:, spots[i]].astype(f32)
        a_all[:, own_cols[i]] = both.astype(bf16)
        g_copies[i].start()
        if i == 0:
            bytes_of(c_bytes, c_recv.at[0]).wait()
            pl.semaphore_wait(whole, n_row + n_col - 2)
        backward(side * halves + i)
    for i in range(halves):
        g_copies[i].wait_recv()
        backward((1 - side) * halves + i)

    def forward(step):
        return jnp.dot(a_all[block(peer("col", step)), :], col_side[...], preferred_element_type=f32)

    bytes_of(r_bytes, r_recv.at[0]).wait()
    for s in range(1, n_col):
        sums[n_row - 1 + s] = forward(s).astype(bf16)
        for target in targets:
            if target[0] == n_row - 1 + s:
                gift(*target).start()
    sums[0] = (own[...] + forward(0)).astype(bf16)
    for target in targets:
        if target[0] == 0:
            gift(*target).start()
    kept = pl.ds(pl.multiple_of(feat * out_rows, out_rows), out_rows)
    gathered[0, :, lanes] = sums[0, kept, :]
    few = pl.ds(0, (n_feat - 1) * out_rows)
    many = pl.ds(1, n_row + n_col - 2)
    bytes_of(part_in.at[pl.ds(1, n_feat - 1)], h_send.at[0]).wait()
    bytes_of(r_bytes, r_send.at[0]).wait()
    bytes_of(c_bytes, c_send.at[0]).wait()
    for copy in n_copies + x_copies + g_copies:
        copy.wait_send()
    bytes_of(sums.at[many], o_send.at[1]).wait()
    bytes_of(sums.at[0, few], o_send.at[0]).wait()
    bytes_of(gathered.at[many], o_recv.at[1]).wait()
    bytes_of(sums.at[0, few], o_recv.at[0]).wait()


def shards(sizes, features, weight, tile_rows, tile_cols, tile_weights, tile_counts):
    n_row, n_col, n_feat = sizes
    pages, depth = features.shape
    width = weight.shape[1]
    slots, tile = tile_weights.shape[2], tile_weights.shape[3]
    share = width // n_feat
    block_rows, block_cols = n_col * tile, n_row * tile
    half = block_cols // 2
    ways = n_row + n_col - 1
    bf16 = jnp.bfloat16
    dma = pltpu.SemaphoreType.DMA
    hbm = pl.BlockSpec(memory_space=pltpu.HBM)
    vmem = pl.BlockSpec(memory_space=pltpu.VMEM)
    rows_c, cols_c, x_c, w_c, t_c = (pltpu.with_memory_space_constraint(a, pltpu.HBM) for a in (tile_rows, tile_cols, features, weight, tile_weights.reshape(slots, tile, tile)))
    gathered = pl.pallas_call(
        functools.partial(layer, sizes),
        out_shape=jax.ShapeDtypeStruct((ways, pages // n_feat, width), bf16),
        in_specs=[hbm] * 6,
        out_specs=vmem,
        scratch_shapes=[
            pltpu.SMEM(tile_rows.shape, jnp.int32),
            pltpu.SMEM(tile_cols.shape, jnp.int32),
            pltpu.SMEM(tile_counts.shape, jnp.int32),
            pltpu.SMEM((slots,), jnp.int32),
            pltpu.SMEM((CHAINS * n_row * n_col,), jnp.int32),
            [pltpu.VMEM((slots // CHAINS + 1, tile, tile), jnp.float32)] * CHAINS,
            pltpu.VMEM((pages, depth), bf16),
            pltpu.VMEM((depth, width), bf16),
            pltpu.VMEM((slots, tile, tile), bf16),
            pltpu.VMEM((n_feat, pages, share), bf16),
            pltpu.VMEM((pages, share), jnp.float32),
            pltpu.VMEM((n_feat, pages, share), bf16),
            pltpu.VMEM((block_cols, share), bf16),
            pltpu.VMEM((block_rows, share), bf16),
            pltpu.VMEM((block_rows, block_cols), bf16),
            pltpu.VMEM((block_rows, half), bf16),
            pltpu.VMEM((block_rows, half), bf16),
            pltpu.VMEM((block_rows, half), bf16),
            pltpu.VMEM((block_rows, block_cols), bf16),
            pltpu.VMEM((tile, share), jnp.float32),
            pltpu.VMEM((ways, pages, share), bf16),
            pltpu.SemaphoreType.REGULAR((n_row,)),
            pltpu.SemaphoreType.REGULAR((n_row,)),
            pltpu.SemaphoreType.REGULAR,
            dma((6,)),
            dma((1,)), dma((1,)),
            dma((n_row // 2,)), dma((n_row // 2,)),
            dma((n_row // 2,)), dma((n_row // 2,)),
            dma((n_row // 2,)), dma((n_row // 2,)),
            dma((1,)), dma((1,)),
            dma((1,)), dma((1,)),
            dma((2,)), dma((2,)),
        ],
        compiler_params=pltpu.CompilerParams(
            collective_id=0, has_side_effects=True, vmem_limit_bytes=24 * 1024 * 1024
        ),
        name="layer",
    )(rows_c, cols_c, tile_counts, x_c, w_c, t_c)
    return jnp.sum(gathered.astype(jnp.float32), axis=0).astype(bf16)


def solution(mesh):
    sizes = tuple(mesh.shape[axis] for axis in ("row", "col", "feat"))
    placed = (
        P(("row", "col"), "feat"),
        P(),
        P("row", "col", "feat"),
        P("row", "col", "feat"),
        P("row", "col", "feat", None, None),
        P("row", "col", "feat"),
    )
    return jax.shard_map(
        functools.partial(shards, sizes),
        mesh=mesh,
        in_specs=placed,
        out_specs=P(("row", "col", "feat"), None),
        check_vma=False,
    )
```

```python
import functools

import jax
import jax.numpy as jnp
from jax import lax
from jax.experimental import pallas as pl
from jax.experimental.pallas import tpu as pltpu
from jax.sharding import PartitionSpec as P

MESH = pl.DeviceIdType.MESH
GROUP = 8
CHAINS = 2


def layer(
    sizes,
    rows_hbm, cols_hbm, count_ref, x_hbm, w_hbm, t_hbm,
    out_ref,
    rows_ref, cols_ref, prev_ref, last_ref, runs,
    x, w, tiles, part, part_own, part_in, col_side, row_side,
    a_part, a_near, a_pair, a_far, a_all, own, sums, gathered,
    known_up, known_down, whole, load_sem, h_send, h_recv, n_send, n_recv, x_send, x_recv, g_send, g_recv,
    r_send, r_recv, c_send, c_recv, o_send, o_recv,
):
    n_row, n_col, n_feat = sizes
    row, col, feat = lax.axis_index("row"), lax.axis_index("col"), lax.axis_index("feat")
    me = {"row": row, "col": col, "feat": feat}
    size = {"row": n_row, "col": n_col, "feat": n_feat}

    def peer(axis, step):
        return lax.rem(me[axis] + step, size[axis])

    def others(axis):
        at, n = me[axis], size[axis]
        upper = (2 * at) // n
        found = []
        for j in range(n - 1):
            down = n - 1 - j
            down = down - (at - down + n) // n
            up = j + (j - at + n) // n
            found.append((1 - upper) * down + upper * up)
        return found

    def remote(to, src, dst, send, recv):
        return pltpu.make_async_remote_copy(
            src_ref=src, dst_ref=dst, send_sem=send, recv_sem=recv,
            device_id=to, device_id_type=MESH,
        )

    slots, tile = tiles.shape[0], tiles.shape[1]
    pages, depth = x.shape
    share = part.shape[2]
    block_rows, half = a_near.shape
    out_rows = out_ref.shape[0]
    f32, bf16 = jnp.float32, jnp.bfloat16

    order = [2, 3, 0, 1] if n_feat == 4 else list(range(n_feat))
    if n_feat == 4:
        mate = feat + 1 - 2 * (feat % 2)
        in_feat = [feat, mate, lax.rem(feat + 2, 4), lax.rem(mate + 2, 4)]
    else:
        in_feat = [peer("feat", t) for t in range(n_feat)]

    targets = []
    for s in range(1, n_row):
        targets += [(s, t, {"row": peer("row", s), "feat": in_feat[t]}) for t in order]
    for s in range(1, n_col):
        targets += [
            (n_row - 1 + s, t, {"col": peer("col", s), "feat": in_feat[t]})
            for t in order
        ]
    targets += [(0, t, {"feat": in_feat[t]}) for t in order if t]

    below, above = row - 1, row + 1
    has_below, has_above = row > 0, row < n_row - 1
    partners = [{"feat": in_feat[t]} for t in order if t]
    partners += [{"col": peer("col", s)} for s in range(1, n_col)]
    greeted = len(partners) + jnp.where(has_below, 1, 0) + jnp.where(has_above, 1, 0)
    def signal(sem, to):
        pl.semaphore_signal(sem, inc=1, device_id=to, device_id_type=MESH)

    def announce():
        @pl.when(has_below & has_above)
        def _():
            signal(known_up.at[2], {"row": above})
            signal(known_down.at[2], {"row": below})

    def hand_on():
        for j in range(2, n_row - 1):
            @pl.when((row >= j) & has_above)
            def _():
                pl.semaphore_wait(known_up.at[j], 1)
                signal(known_up.at[j + 1], {"row": above})

            @pl.when((row + j < n_row) & has_below)
            def _():
                pl.semaphore_wait(known_down.at[j], 1)
                signal(known_down.at[j + 1], {"row": below})

    def learn():
        for j in range(2, n_row):
            @pl.when((row >= j) & (row == n_row - 1))
            def _():
                pl.semaphore_wait(known_up.at[j], 1)

            @pl.when((row + j < n_row) & (row == 0))
            def _():
                pl.semaphore_wait(known_down.at[j], 1)
        for s in range(1, n_row):
            signal(whole, {"row": peer("row", s)})
        for s in range(1, n_col):
            signal(whole, {"col": peer("col", s)})

    loads = [
        pltpu.make_async_copy(x_hbm, x, load_sem.at[0]),
        pltpu.make_async_copy(
            w_hbm.at[pl.ds(pl.multiple_of(feat * depth, depth), depth)], w, load_sem.at[1]
        ),
        pltpu.make_async_copy(rows_hbm, rows_ref, load_sem.at[2]),
        pltpu.make_async_copy(cols_hbm, cols_ref, load_sem.at[3]),
        pltpu.make_async_copy(t_hbm, tiles, load_sem.at[4]),
    ]
    for load in loads[:2]:
        load.start()
    barrier = pltpu.get_barrier_semaphore()
    for to in partners:
        signal(barrier, to)

    @pl.when(has_below)
    def _():
        signal(barrier, {"row": below})

    @pl.when(has_above)
    def _():
        signal(barrier, {"row": above})

    for load in loads[2:]:
        load.start()

    loads[0].wait()
    loads[1].wait()

    def h_copy(s):
        to = in_feat[s]
        return remote({"feat": to}, part.at[to], part_in.at[s], h_send.at[0], h_recv.at[0])

    def bytes_of(ref, sem):
        return pltpu.make_async_copy(ref, ref, sem)

    def product(s):
        lanes = pl.ds(pl.multiple_of(in_feat[s] * share, share), share)
        return jnp.dot(x[...], w[:, lanes], preferred_element_type=f32)

    h_order = [s for s in order if s]
    for s in h_order:
        part[in_feat[s]] = product(s).astype(bf16)
    pl.semaphore_wait(barrier, greeted)
    for s in h_order:
        h_copy(s).start()
    announce()
    part_own[...] = product(0)
    for load in loads[2:4]:
        load.wait()
    count = count_ref[0, 0, 0]
    row_tiles, col_tiles = n_col, n_row
    places = row_tiles * col_tiles
    chain = slots // len(runs)

    def link(k, last):
        place = cols_ref[0, 0, k] * row_tiles + rows_ref[0, 0, k]
        live = jnp.where(k < count, place, -1)
        before = jnp.int32(0)
        for q in range(places):
            before = jnp.where(place == q, last[q], before)
        prev_ref[k] = before
        return tuple(jnp.where(live == q, k % chain + 1, last[q]) for q in range(places))

    for c, run in enumerate(runs):
        run[0] = jnp.zeros((tile, tile), f32)
        last = lax.fori_loop(
            c * chain, (c + 1) * chain, link, (jnp.int32(0),) * places, unroll=chain if places <= GROUP else 1
        )
        for q in range(places):
            last_ref[c * places + q] = last[q]
    loads[4].wait()

    def add_slots(k, carry):
        values = [
            tiles[c * chain + k].astype(f32) + run[prev_ref[c * chain + k]]
            for c, run in enumerate(runs)
        ]
        for run, value in zip(runs, values):
            run[k + 1] = value
        return carry

    lax.fori_loop(0, chain, add_slots, 0, unroll=4)

    def place_sum(q, carry):
        value = runs[0][last_ref[q]]
        for c in range(1, len(runs)):
            value += runs[c][last_ref[c * places + q]]
        at_col = pl.multiple_of((q // row_tiles) * tile, tile)
        at_row = pl.multiple_of((q % row_tiles) * tile, tile)
        a_part[pl.ds(at_row, tile), pl.ds(at_col, tile)] = value.astype(bf16)
        return carry

    lax.fori_loop(0, places, place_sum, 0, unroll=GROUP)

    side = feat % 2
    near, far = {"feat": feat + 1 - 2 * side}, {"feat": lax.rem(feat + 2, n_feat)}
    halves = half // tile
    near_cols = [pl.ds(pl.multiple_of((1 - side) * half + i * tile, tile), tile) for i in range(halves)]
    own_cols = [pl.ds(pl.multiple_of(side * half + i * tile, tile), tile) for i in range(halves)]
    spots = [pl.ds(i * tile, tile) for i in range(halves)]
    n_copies = [
        remote(near, a_part.at[:, near_cols[i]], a_near.at[:, spots[i]], n_send.at[i], n_recv.at[i])
        for i in range(halves)
    ]
    x_copies = [
        remote(far, a_pair.at[:, spots[i]], a_far.at[:, spots[i]], x_send.at[i], x_recv.at[i])
        for i in range(halves)
    ]
    g_copies = [
        remote(near, a_all.at[:, own_cols[i]], a_all.at[:, own_cols[i]], g_send.at[i], g_recv.at[i])
        for i in range(halves)
    ]
    for copy in n_copies:
        copy.start()
    for i in range(halves):
        n_copies[i].wait_recv()
        pair = a_part[:, own_cols[i]].astype(f32) + a_near[:, spots[i]].astype(f32)
        a_pair[:, spots[i]] = pair.astype(bf16)
        x_copies[i].start()

    hand_on()
    learn()

    def block(at):
        return pl.ds(pl.multiple_of(at * tile, tile), tile)

    bytes_of(part_in.at[pl.ds(1, n_feat - 1)], h_recv.at[0]).wait()
    hidden = part_own[...]
    for s in range(1, n_feat):
        hidden += part_in[s].astype(f32)
    hidden = hidden.astype(bf16)
    col_side[block(row), :] = hidden
    row_side[block(col), :] = hidden
    for at in others("row"):
        spot = col_side.at[block(row)]
        remote({"row": at}, spot, spot, r_send.at[0], r_recv.at[0]).start()
    for s in range(1, n_col):
        spot = row_side.at[block(col)]
        remote({"col": peer("col", s)}, spot, spot, c_send.at[0], c_recv.at[0]).start()
    r_bytes = col_side.at[pl.ds(0, (n_row - 1) * tile)]
    c_bytes = row_side.at[pl.ds(0, (n_col - 1) * tile)]

    lanes = pl.ds(pl.multiple_of(feat * share, share), share)

    def gift(slot, t, to):
        kind = 0 if isinstance(slot, int) and slot == 0 else 1
        rows = pl.ds(pl.multiple_of(in_feat[t] * out_rows, out_rows), out_rows)
        return remote(
            to, sums.at[slot, rows], gathered.at[slot, :, lanes],
            o_send.at[kind], o_recv.at[kind],
        )

    def backward(at):
        cols = pl.ds(pl.multiple_of(at * tile, tile), tile)
        value = lax.dot_general(
            a_all[:, cols], row_side[...], (((0,), (0,)), ((), ())), preferred_element_type=f32
        )
        slot = lax.rem(at - row + n_row, n_row)

        @pl.when(slot == 0)
        def _():
            own[...] = value

        @pl.when(slot != 0)
        def _():
            sums[slot] = value.astype(bf16)
            for t in order:
                gift(slot, t, {"row": at, "feat": in_feat[t]}).start()

    for i in range(halves):
        x_copies[i].wait_recv()
        both = a_pair[:, spots[i]].astype(f32) + a_far[:, spots[i]].astype(f32)
        a_all[:, own_cols[i]] = both.astype(bf16)
        g_copies[i].start()
        if i == 0:
            bytes_of(c_bytes, c_recv.at[0]).wait()
            pl.semaphore_wait(whole, n_row + n_col - 2)
        backward(side * halves + i)
    for i in range(halves):
        g_copies[i].wait_recv()
        backward((1 - side) * halves + i)

    def forward(step, at):
        return jnp.dot(
            a_all[block(peer("col", step)), block(at)], col_side[block(at), :], preferred_element_type=f32
        )

    steps = [*range(1, n_col), 0]
    totals = [forward(s, row) for s in steps]
    totals[-1] += own[...]
    bytes_of(r_bytes, r_recv.at[0]).wait()
    for i, s in enumerate(steps):
        for at in others("row"):
            totals[i] += forward(s, at)
        slot = n_row - 1 + s if s else 0
        sums[slot] = totals[i].astype(bf16)
        for target in targets:
            if target[0] == slot:
                gift(*target).start()
    kept = pl.ds(pl.multiple_of(feat * out_rows, out_rows), out_rows)
    gathered[0, :, lanes] = sums[0, kept, :]
    few = pl.ds(0, (n_feat - 1) * out_rows)
    many = pl.ds(1, n_row + n_col - 2)
    bytes_of(part_in.at[pl.ds(1, n_feat - 1)], h_send.at[0]).wait()
    bytes_of(r_bytes, r_send.at[0]).wait()
    bytes_of(c_bytes, c_send.at[0]).wait()
    for copy in n_copies + x_copies + g_copies:
        copy.wait_send()
    bytes_of(sums.at[many], o_send.at[1]).wait()
    bytes_of(sums.at[0, few], o_send.at[0]).wait()
    bytes_of(gathered.at[many], o_recv.at[1]).wait()
    bytes_of(sums.at[0, few], o_recv.at[0]).wait()
    total = gathered[0].astype(f32)
    for slot in range(1, n_row + n_col - 1):
        total += gathered[slot].astype(f32)
    out_ref[...] = total.astype(bf16)


def shards(sizes, features, weight, tile_rows, tile_cols, tile_weights, tile_counts):
    n_row, n_col, n_feat = sizes
    pages, depth = features.shape
    width = weight.shape[1]
    slots, tile = tile_weights.shape[2], tile_weights.shape[3]
    share = width // n_feat
    block_rows, block_cols = n_col * tile, n_row * tile
    half = block_cols // 2
    ways = n_row + n_col - 1
    bf16 = jnp.bfloat16
    dma = pltpu.SemaphoreType.DMA
    hbm = pl.BlockSpec(memory_space=pltpu.HBM)
    vmem = pl.BlockSpec(memory_space=pltpu.VMEM)
    rows_c, cols_c, x_c, w_c, t_c = (pltpu.with_memory_space_constraint(a, pltpu.HBM) for a in (tile_rows, tile_cols, features, weight, tile_weights.reshape(slots, tile, tile)))
    return pl.pallas_call(
        functools.partial(layer, sizes),
        out_shape=jax.ShapeDtypeStruct((pages // n_feat, width), bf16),
        in_specs=[hbm] * 2 + [pl.BlockSpec(memory_space=pltpu.SMEM)] + [hbm] * 3,
        out_specs=vmem,
        scratch_shapes=[
            pltpu.SMEM(tile_rows.shape, jnp.int32),
            pltpu.SMEM(tile_cols.shape, jnp.int32),
            pltpu.SMEM((slots,), jnp.int32),
            pltpu.SMEM((CHAINS * n_row * n_col,), jnp.int32),
            [pltpu.VMEM((slots // CHAINS + 1, tile, tile), jnp.float32)] * CHAINS,
            pltpu.VMEM((pages, depth), bf16),
            pltpu.VMEM((depth, width), bf16),
            pltpu.VMEM((slots, tile, tile), bf16),
            pltpu.VMEM((n_feat, pages, share), bf16),
            pltpu.VMEM((pages, share), jnp.float32),
            pltpu.VMEM((n_feat, pages, share), bf16),
            pltpu.VMEM((block_cols, share), bf16),
            pltpu.VMEM((block_rows, share), bf16),
            pltpu.VMEM((block_rows, block_cols), bf16),
            pltpu.VMEM((block_rows, half), bf16),
            pltpu.VMEM((block_rows, half), bf16),
            pltpu.VMEM((block_rows, half), bf16),
            pltpu.VMEM((block_rows, block_cols), bf16),
            pltpu.VMEM((tile, share), jnp.float32),
            pltpu.VMEM((ways, pages, share), bf16),
            pltpu.VMEM((ways, pages // n_feat, width), bf16),
            pltpu.SemaphoreType.REGULAR((n_row,)),
            pltpu.SemaphoreType.REGULAR((n_row,)),
            pltpu.SemaphoreType.REGULAR,
            dma((5,)),
            dma((1,)), dma((1,)),
            dma((n_row // 2,)), dma((n_row // 2,)),
            dma((n_row // 2,)), dma((n_row // 2,)),
            dma((n_row // 2,)), dma((n_row // 2,)),
            dma((1,)), dma((1,)),
            dma((1,)), dma((1,)),
            dma((2,)), dma((2,)),
        ],
        compiler_params=pltpu.CompilerParams(
            collective_id=0, has_side_effects=True, vmem_limit_bytes=24 * 1024 * 1024
        ),
        name="layer",
    )(rows_c, cols_c, tile_counts, x_c, w_c, t_c)


def solution(mesh):
    sizes = tuple(mesh.shape[axis] for axis in ("row", "col", "feat"))
    placed = (
        P(("row", "col"), "feat"),
        P(),
        P("row", "col", "feat"),
        P("row", "col", "feat"),
        P("row", "col", "feat", None, None),
        P("row", "col", "feat"),
    )
    return jax.shard_map(
        functools.partial(shards, sizes),
        mesh=mesh,
        in_specs=placed,
        out_specs=P(("row", "col", "feat"), None),
        check_vma=False,
    )
```

```python
import functools

import jax
import jax.numpy as jnp
from jax import lax
from jax.experimental import pallas as pl
from jax.experimental.pallas import tpu as pltpu
from jax.sharding import PartitionSpec as P

MESH = pl.DeviceIdType.MESH
GROUP = 8
CHAINS = 2


def layer(
    sizes,
    rows_hbm, cols_hbm, count_hbm, x_hbm, w_hbm, t_hbm,
    out_ref,
    rows_ref, cols_ref, count_ref, prev_ref, last_ref, runs,
    x, w, tiles, part, part_own, part_in, col_side, row_side,
    a_part, a_near, a_pair, a_far, a_all, own, sums, gathered,
    known_up, known_down, whole, load_sem, h_send, h_recv, n_send, n_recv, x_send, x_recv, g_send, g_recv,
    r_send, r_recv, c_send, c_recv, o_send, o_recv,
):
    n_row, n_col, n_feat = sizes
    row, col, feat = lax.axis_index("row"), lax.axis_index("col"), lax.axis_index("feat")
    me = {"row": row, "col": col, "feat": feat}
    size = {"row": n_row, "col": n_col, "feat": n_feat}

    def peer(axis, step):
        return lax.rem(me[axis] + step, size[axis])

    def others(axis):
        at, n = me[axis], size[axis]
        upper = (2 * at) // n
        found = []
        for j in range(n - 1):
            down = n - 1 - j
            down = down - (at - down + n) // n
            up = j + (j - at + n) // n
            found.append((1 - upper) * down + upper * up)
        return found

    def remote(to, src, dst, send, recv):
        return pltpu.make_async_remote_copy(
            src_ref=src, dst_ref=dst, send_sem=send, recv_sem=recv,
            device_id=to, device_id_type=MESH,
        )

    slots, tile = tiles.shape[0], tiles.shape[1]
    pages, depth = x.shape
    share = part.shape[2]
    block_rows, half = a_near.shape
    out_rows = out_ref.shape[0]
    f32, bf16 = jnp.float32, jnp.bfloat16

    targets = []
    for s in range(1, n_row):
        targets += [(s, t, {"row": peer("row", s), "feat": peer("feat", t)}) for t in range(n_feat)]
    for s in range(1, n_col):
        targets += [
            (n_row - 1 + s, t, {"col": peer("col", s), "feat": peer("feat", t)})
            for t in range(n_feat)
        ]
    targets += [(0, t, {"feat": peer("feat", t)}) for t in range(1, n_feat)]

    below, above = row - 1, row + 1
    has_below, has_above = row > 0, row < n_row - 1
    partners = [{"feat": peer("feat", t)} for t in range(1, n_feat)]
    partners += [{"col": peer("col", s)} for s in range(1, n_col)]
    greeted = len(partners) + jnp.where(has_below, 1, 0) + jnp.where(has_above, 1, 0)
    def signal(sem, to):
        pl.semaphore_signal(sem, inc=1, device_id=to, device_id_type=MESH)

    def announce():
        @pl.when(has_below & has_above)
        def _():
            signal(known_up.at[2], {"row": above})
            signal(known_down.at[2], {"row": below})

    def hand_on():
        for j in range(2, n_row - 1):
            @pl.when((row >= j) & has_above)
            def _():
                pl.semaphore_wait(known_up.at[j], 1)
                signal(known_up.at[j + 1], {"row": above})

            @pl.when((row + j < n_row) & has_below)
            def _():
                pl.semaphore_wait(known_down.at[j], 1)
                signal(known_down.at[j + 1], {"row": below})

    def learn():
        for j in range(2, n_row):
            @pl.when((row >= j) & (row == n_row - 1))
            def _():
                pl.semaphore_wait(known_up.at[j], 1)

            @pl.when((row + j < n_row) & (row == 0))
            def _():
                pl.semaphore_wait(known_down.at[j], 1)
        for s in range(1, n_row):
            signal(whole, {"row": peer("row", s)})
        for s in range(1, n_col):
            signal(whole, {"col": peer("col", s)})

    loads = [
        pltpu.make_async_copy(x_hbm, x, load_sem.at[0]),
        pltpu.make_async_copy(
            w_hbm.at[pl.ds(pl.multiple_of(feat * depth, depth), depth)], w, load_sem.at[1]
        ),
        pltpu.make_async_copy(rows_hbm, rows_ref, load_sem.at[2]),
        pltpu.make_async_copy(cols_hbm, cols_ref, load_sem.at[3]),
        pltpu.make_async_copy(count_hbm, count_ref, load_sem.at[4]),
        pltpu.make_async_copy(t_hbm, tiles, load_sem.at[5]),
    ]
    for load in loads[:2]:
        load.start()
    barrier = pltpu.get_barrier_semaphore()
    for to in partners:
        signal(barrier, to)

    @pl.when(has_below)
    def _():
        signal(barrier, {"row": below})

    @pl.when(has_above)
    def _():
        signal(barrier, {"row": above})

    for load in loads[2:]:
        load.start()

    loads[0].wait()
    loads[1].wait()

    def h_copy(s):
        to = peer("feat", s)
        return remote({"feat": to}, part.at[to], part_in.at[s], h_send.at[0], h_recv.at[0])

    def bytes_of(ref, sem):
        return pltpu.make_async_copy(ref, ref, sem)

    def product(s):
        lanes = pl.ds(pl.multiple_of(peer("feat", s) * share, share), share)
        return jnp.dot(x[...], w[:, lanes], preferred_element_type=f32)

    h_order = [2, 1, 3] if n_feat == 4 else list(range(1, n_feat))
    for s in h_order:
        part[peer("feat", s)] = product(s).astype(bf16)
    pl.semaphore_wait(barrier, greeted)
    for s in h_order:
        h_copy(s).start()
    announce()
    part_own[...] = product(0)
    for load in loads[2:5]:
        load.wait()
    count = count_ref[0, 0, 0]
    row_tiles, col_tiles = n_col, n_row
    places = row_tiles * col_tiles
    chain = slots // len(runs)

    def link(k, last):
        place = cols_ref[0, 0, k] * row_tiles + rows_ref[0, 0, k]
        live = jnp.where(k < count, place, -1)
        before = jnp.int32(0)
        for q in range(places):
            before = jnp.where(place == q, last[q], before)
        prev_ref[k] = before
        return tuple(jnp.where(live == q, k % chain + 1, last[q]) for q in range(places))

    for c, run in enumerate(runs):
        run[0] = jnp.zeros((tile, tile), f32)
        last = lax.fori_loop(
            c * chain, (c + 1) * chain, link, (jnp.int32(0),) * places, unroll=chain if places <= GROUP else 1
        )
        for q in range(places):
            last_ref[c * places + q] = last[q]
    loads[5].wait()

    def add_slots(k, carry):
        values = [
            tiles[c * chain + k].astype(f32) + run[prev_ref[c * chain + k]]
            for c, run in enumerate(runs)
        ]
        for run, value in zip(runs, values):
            run[k + 1] = value
        return carry

    lax.fori_loop(0, chain, add_slots, 0, unroll=4)

    def place_sum(q, carry):
        value = runs[0][last_ref[q]]
        for c in range(1, len(runs)):
            value += runs[c][last_ref[c * places + q]]
        at_col = pl.multiple_of((q // row_tiles) * tile, tile)
        at_row = pl.multiple_of((q % row_tiles) * tile, tile)
        a_part[pl.ds(at_row, tile), pl.ds(at_col, tile)] = value.astype(bf16)
        return carry

    lax.fori_loop(0, places, place_sum, 0, unroll=GROUP)

    side = feat % 2
    near, far = {"feat": feat + 1 - 2 * side}, {"feat": lax.rem(feat + 2, n_feat)}
    halves = half // tile
    near_cols = [pl.ds(pl.multiple_of((1 - side) * half + i * tile, tile), tile) for i in range(halves)]
    own_cols = [pl.ds(pl.multiple_of(side * half + i * tile, tile), tile) for i in range(halves)]
    spots = [pl.ds(i * tile, tile) for i in range(halves)]
    n_copies = [
        remote(near, a_part.at[:, near_cols[i]], a_near.at[:, spots[i]], n_send.at[i], n_recv.at[i])
        for i in range(halves)
    ]
    x_copies = [
        remote(far, a_pair.at[:, spots[i]], a_far.at[:, spots[i]], x_send.at[i], x_recv.at[i])
        for i in range(halves)
    ]
    g_copies = [
        remote(near, a_all.at[:, own_cols[i]], a_all.at[:, own_cols[i]], g_send.at[i], g_recv.at[i])
        for i in range(halves)
    ]
    for copy in n_copies:
        copy.start()
    for i in range(halves):
        n_copies[i].wait_recv()
        pair = a_part[:, own_cols[i]].astype(f32) + a_near[:, spots[i]].astype(f32)
        a_pair[:, spots[i]] = pair.astype(bf16)
        x_copies[i].start()

    hand_on()
    learn()

    def block(at):
        return pl.ds(pl.multiple_of(at * tile, tile), tile)

    bytes_of(part_in.at[pl.ds(1, n_feat - 1)], h_recv.at[0]).wait()
    hidden = part_own[...]
    for s in range(1, n_feat):
        hidden += part_in[s].astype(f32)
    hidden = hidden.astype(bf16)
    col_side[block(row), :] = hidden
    row_side[block(col), :] = hidden
    for s in range(1, n_col):
        spot = row_side.at[block(col)]
        remote({"col": peer("col", s)}, spot, spot, c_send.at[0], c_recv.at[0]).start()
    for at in others("row"):
        spot = col_side.at[block(row)]
        remote({"row": at}, spot, spot, r_send.at[0], r_recv.at[0]).start()
    r_bytes = col_side.at[pl.ds(0, (n_row - 1) * tile)]
    c_bytes = row_side.at[pl.ds(0, (n_col - 1) * tile)]

    lanes = pl.ds(pl.multiple_of(feat * share, share), share)

    def gift(slot, t, to):
        kind = 0 if isinstance(slot, int) and slot == 0 else 1
        rows = pl.ds(pl.multiple_of(peer("feat", t) * out_rows, out_rows), out_rows)
        return remote(
            to, sums.at[slot, rows], gathered.at[slot, :, lanes],
            o_send.at[kind], o_recv.at[kind],
        )

    def backward(at):
        cols = pl.ds(pl.multiple_of(at * tile, tile), tile)
        value = lax.dot_general(
            a_all[:, cols], row_side[...], (((0,), (0,)), ((), ())), preferred_element_type=f32
        )
        slot = lax.rem(at - row + n_row, n_row)

        @pl.when(slot == 0)
        def _():
            own[...] = value

        @pl.when(slot != 0)
        def _():
            sums[slot] = value.astype(bf16)
            for t in range(n_feat):
                gift(slot, t, {"row": at, "feat": peer("feat", t)}).start()

    for i in range(halves):
        x_copies[i].wait_recv()
        both = a_pair[:, spots[i]].astype(f32) + a_far[:, spots[i]].astype(f32)
        a_all[:, own_cols[i]] = both.astype(bf16)
        g_copies[i].start()
        if i == 0:
            bytes_of(c_bytes, c_recv.at[0]).wait()
            pl.semaphore_wait(whole, n_row + n_col - 2)
        backward(side * halves + i)
    for i in range(halves):
        g_copies[i].wait_recv()
        backward((1 - side) * halves + i)

    def forward(step):
        return jnp.dot(a_all[block(peer("col", step)), :], col_side[...], preferred_element_type=f32)

    bytes_of(r_bytes, r_recv.at[0]).wait()
    for s in range(1, n_col):
        sums[n_row - 1 + s] = forward(s).astype(bf16)
        for target in targets:
            if target[0] == n_row - 1 + s:
                gift(*target).start()
    sums[0] = (own[...] + forward(0)).astype(bf16)
    for target in targets:
        if target[0] == 0:
            gift(*target).start()
    kept = pl.ds(pl.multiple_of(feat * out_rows, out_rows), out_rows)
    gathered[0, :, lanes] = sums[0, kept, :]
    few = pl.ds(0, (n_feat - 1) * out_rows)
    many = pl.ds(1, n_row + n_col - 2)
    bytes_of(part_in.at[pl.ds(1, n_feat - 1)], h_send.at[0]).wait()
    bytes_of(r_bytes, r_send.at[0]).wait()
    bytes_of(c_bytes, c_send.at[0]).wait()
    for copy in n_copies + x_copies + g_copies:
        copy.wait_send()
    bytes_of(gathered.at[many], o_recv.at[1]).wait()
    bytes_of(sums.at[0, few], o_recv.at[0]).wait()
    total = gathered[0].astype(f32)
    for slot in range(1, n_row + n_col - 1):
        total += gathered[slot].astype(f32)
    out_ref[...] = total.astype(bf16)
    bytes_of(sums.at[many], o_send.at[1]).wait()
    bytes_of(sums.at[0, few], o_send.at[0]).wait()


def shards(sizes, features, weight, tile_rows, tile_cols, tile_weights, tile_counts):
    n_row, n_col, n_feat = sizes
    pages, depth = features.shape
    width = weight.shape[1]
    slots, tile = tile_weights.shape[2], tile_weights.shape[3]
    share = width // n_feat
    block_rows, block_cols = n_col * tile, n_row * tile
    half = block_cols // 2
    ways = n_row + n_col - 1
    bf16 = jnp.bfloat16
    dma = pltpu.SemaphoreType.DMA
    hbm = pl.BlockSpec(memory_space=pltpu.HBM)
    vmem = pl.BlockSpec(memory_space=pltpu.VMEM)
    rows_c, cols_c, x_c, w_c, t_c = (pltpu.with_memory_space_constraint(a, pltpu.HBM) for a in (tile_rows, tile_cols, features, weight, tile_weights.reshape(slots, tile, tile)))
    return pl.pallas_call(
        functools.partial(layer, sizes),
        out_shape=jax.ShapeDtypeStruct((pages // n_feat, width), bf16),
        in_specs=[hbm] * 6,
        out_specs=vmem,
        scratch_shapes=[
            pltpu.SMEM(tile_rows.shape, jnp.int32),
            pltpu.SMEM(tile_cols.shape, jnp.int32),
            pltpu.SMEM(tile_counts.shape, jnp.int32),
            pltpu.SMEM((slots,), jnp.int32),
            pltpu.SMEM((CHAINS * n_row * n_col,), jnp.int32),
            [pltpu.VMEM((slots // CHAINS + 1, tile, tile), jnp.float32)] * CHAINS,
            pltpu.VMEM((pages, depth), bf16),
            pltpu.VMEM((depth, width), bf16),
            pltpu.VMEM((slots, tile, tile), bf16),
            pltpu.VMEM((n_feat, pages, share), bf16),
            pltpu.VMEM((pages, share), jnp.float32),
            pltpu.VMEM((n_feat, pages, share), bf16),
            pltpu.VMEM((block_cols, share), bf16),
            pltpu.VMEM((block_rows, share), bf16),
            pltpu.VMEM((block_rows, block_cols), bf16),
            pltpu.VMEM((block_rows, half), bf16),
            pltpu.VMEM((block_rows, half), bf16),
            pltpu.VMEM((block_rows, half), bf16),
            pltpu.VMEM((block_rows, block_cols), bf16),
            pltpu.VMEM((tile, share), jnp.float32),
            pltpu.VMEM((ways, pages, share), bf16),
            pltpu.VMEM((ways, pages // n_feat, width), bf16),
            pltpu.SemaphoreType.REGULAR((n_row,)),
            pltpu.SemaphoreType.REGULAR((n_row,)),
            pltpu.SemaphoreType.REGULAR,
            dma((6,)),
            dma((1,)), dma((1,)),
            dma((n_row // 2,)), dma((n_row // 2,)),
            dma((n_row // 2,)), dma((n_row // 2,)),
            dma((n_row // 2,)), dma((n_row // 2,)),
            dma((1,)), dma((1,)),
            dma((1,)), dma((1,)),
            dma((2,)), dma((2,)),
        ],
        compiler_params=pltpu.CompilerParams(
            collective_id=0, has_side_effects=True, vmem_limit_bytes=24 * 1024 * 1024
        ),
        name="layer",
    )(rows_c, cols_c, tile_counts, x_c, w_c, t_c)


def solution(mesh):
    sizes = tuple(mesh.shape[axis] for axis in ("row", "col", "feat"))
    placed = (
        P(("row", "col"), "feat"),
        P(),
        P("row", "col", "feat"),
        P("row", "col", "feat"),
        P("row", "col", "feat", None, None),
        P("row", "col", "feat"),
    )
    return jax.shard_map(
        functools.partial(shards, sizes),
        mesh=mesh,
        in_specs=placed,
        out_specs=P(("row", "col", "feat"), None),
        check_vma=False,
    )
```
